32 devices in a mesh: fsdp: 8 (over y, x, core), tp: 4 (over z).
Axes of the slice: x: 2, y: 2, z: 4, core: 2. Of those that a mesh axis runs over, the one named last changes fastest.
Arguments:
- tokens: bfloat16 [2, 2048, 2048], P(None, ('fsdp', 'tp')), may hold values from -6 to 6
- cotangent: bfloat16 [2, 2048, 2048], P(None, ('fsdp', 'tp')), may hold values from -6 to 6
- lengths: int32 [2, 3], replicated, may hold values from 1 to 1024, 2048 in all within a row
- dealing: int32 [2, 2048], replicated, may hold values from 0 to 2047, each once within a row
- routes: int32 [2, 2048, 8], P(None, 'fsdp'), may hold values from 0 to 63, all different within a row; in each aligned block of 256 rows (0 to 255, 256 to 511, ..., all dimensions but the last counted through in order) at most 48 rows name the same one
- gate_weights: float32 [2, 2048, 8], P(None, 'fsdp'), may hold values from 0.1 to 0.5
- attention_gain: float32 [2048], replicated, may hold values from 0.5 to 1.5
- mixture_gain: float32 [2048], replicated, may hold values from 0.5 to 1.5
- query_gain: float32 [128], replicated, may hold values from 0.5 to 1.5
- key_gain: float32 [128], replicated, may hold values from 0.5 to 1.5
- query_weight: bfloat16 [2048, 2048], P('fsdp', 'tp'), may hold values from -0.125 to 0.125
- key_weight: bfloat16 [2048, 2048], P('fsdp', 'tp'), may hold values from -0.125 to 0.125
- value_weight: bfloat16 [2048, 2048], P('fsdp', 'tp'), may hold values from -0.125 to 0.125
- out_weight: bfloat16 [2048, 2048], P('fsdp', 'tp'), may hold values from -2 to 2
- gate_weight: bfloat16 [64, 2048, 1024], P('fsdp', None, 'tp'), may hold values from -0.125 to 0.125
- up_weight: bfloat16 [64, 2048, 1024], P('fsdp', None, 'tp'), may hold values from -0.125 to 0.125
- down_weight: bfloat16 [64, 1024, 2048], P('fsdp', 'tp'), may hold values from -0.375 to 0.375
Outputs:
- output: bfloat16 [2, 2048, 2048], P(None, ('fsdp', 'tp'))
- input_grad: float32 [2, 2048, 2048], P(None, ('fsdp', 'tp'))
- attention_gain_grad: float32 [2048], replicated
- mixture_gain_grad: float32 [2048], replicated
- query_gain_grad: float32 [128], replicated
- key_gain_grad: float32 [128], replicated
- query_weight_grad: float32 [2048, 2048], P('fsdp', 'tp')
- key_weight_grad: float32 [2048, 2048], P('fsdp', 'tp')
- value_weight_grad: float32 [2048, 2048], P('fsdp', 'tp')
- out_weight_grad: float32 [2048, 2048], P('fsdp', 'tp')
- gate_weight_grad: float32 [64, 2048, 1024], P('fsdp', None, 'tp')
- up_weight_grad: float32 [64, 2048, 1024], P('fsdp', None, 'tp')
- down_weight_grad: float32 [64, 1024, 2048], P('fsdp', 'tp')
The draws below stay inside these ranges and needn't reach their ends.
Inputs may be any that keep to these rules, and one draw needn't show every extreme that they name: `dealing`: each row lists every number of 0 to 2047 once. The 3 lengths of a micro-batch sum to 2048; the longest is 1024. `routes`: A row names 8 different experts. In each aligned block of 256 rows (the rows of one fsdp index in one micro-batch) no expert is named by more than 48 rows, a bound that some block reaches.
All inputs are finite; a program needn't handle non-finite values.
Results may differ from the reference program's by a relative error of at most 0.023.
Values may be sent and summed in bfloat16 or wider, within the bound.
No kernel may reach another device: no remote copies, remote signals or barrier semaphores. Data moves between devices by JAX's collectives and lax.ppermute only.
A program may use at most 448 MiB of HBM per device.

```python
import math
import jax
import jax.numpy as jnp
import numpy as np
from jax import lax

D = 2048
HEADS = 16
HEAD = 128
EXPERTS = 64
FF = 1024
TOPK = 8
TOK = 256
MB = 2
TOKENS = 2048
LMAX = 1024
NSEQ = 3
CAP = 48
N_FSDP = 8
N_TP = 4


def shard_levels(stream_key, shape, split, low, top_value):
    level, own = 1.0, jax.random.fold_in(stream_key, 6)
    for axis_at, shards_of in split:
        steps = jnp.exp(jax.random.uniform(jax.random.fold_in(own, axis_at), (shards_of,), jnp.float32, low / len(split), top_value / len(split)))
        level = level * jnp.repeat(steps, shape[axis_at] // shards_of).reshape([-1 if axis == axis_at else 1 for axis in range(len(shape))])
    return level


def length_profile(amount, total, bound, slope):
    loads = [(1 << 20) // math.isqrt(grade ** slope) + 1 for grade in range(2, amount + 1)]
    spare, holding = total - bound - (amount - 1), [1] * (amount - 1)
    while spare > 0:
        movable = [i for i in range(amount - 1) if holding[i] < bound]
        mass, remaining = sum([loads[i] for i in movable]), spare
        for i in movable:
            addition = min(bound - holding[i], max(1, remaining * loads[i] // mass), spare)
            holding[i] = holding[i] + addition
            spare = spare - addition
    return np.array([bound] + holding)


def uneven_parts(own_key, number_of, total, bound, slope):
    if number_of == 2:
        one = jax.random.randint(own_key, (), max(1, total - bound), min(bound, total - 1) + 1)
        return jnp.stack([one, total - one])
    sizes = jnp.asarray(length_profile(number_of, total, bound, slope), jnp.int32)
    twos = (number_of - 1) // 2
    source_of, receiver = sizes[1:1 + 2 * twos:2], sizes[2:2 + 2 * twos:2]
    room = jnp.minimum(source_of - 1, bound - receiver)
    moved = jax.random.randint(jax.random.fold_in(own_key, 1), (twos,), 0, 1 << 20) % (room + 1)
    sizes = sizes.at[1:1 + 2 * twos:2].set(source_of - moved).at[2:2 + 2 * twos:2].set(receiver + moved)
    return sizes[jax.random.permutation(jax.random.fold_in(own_key, 2), number_of)]


def deal_out(stream_key, own, number, rows, number_of, top, limit, lean):
    ranking = jax.random.permutation(stream_key, number_of)
    crowded, common = portions_of(number_of, rows * top, limit, lean, True), portions_of(number_of, rows * top, limit, lean, False)
    places = jnp.arange(number_of)

    def named(sizes, offset_by):
        used = int((sizes > 0).sum())
        fixed = max(1, used // 4)
        moved = fixed + (places - fixed + offset_by * (used - fixed)) % max(1, number_of - fixed)
        return jnp.zeros((number_of,), jnp.int32).at[ranking[jnp.where(places < fixed, places, moved)]].set(jnp.asarray(sizes, jnp.int32))

    sizes = jnp.where(number % 4 == 0, named(crowded, number // 4), named(common, number - number // 4 - 1))
    mixed = jax.random.permutation(jax.random.fold_in(own, 3), number_of)
    donor, taker = mixed[0:number_of // 2 * 2:2], mixed[1:number_of // 2 * 2:2]
    room = jnp.minimum(sizes[donor] - 1, limit - sizes[taker]) // 2
    room = jnp.where((donor == ranking[0]) | (taker == ranking[0]) | (sizes[taker] == 0), 0, jnp.maximum(room, 0))
    moved = jax.random.randint(jax.random.fold_in(own, 4), (number_of // 2,), 0, 1 << 20) % (room + 1)
    sizes = sizes.at[donor].add(-moved).at[taker].add(moved)
    items = jnp.searchsorted(jnp.cumsum(sizes), jnp.arange(rows * top), side="right").astype(jnp.int32)
    table = items.reshape(top, rows).T
    table = table[jax.random.permutation(jax.random.fold_in(own, 1), rows)]
    offset_by = jax.random.randint(jax.random.fold_in(own, 2), (rows, 1), 0, top)
    return jnp.take_along_axis(table, (jnp.arange(top)[None, :] + offset_by) % top, axis=1)


def portions_of(count, total, limit, skew, full):
    weights = [(1 << 20) // math.isqrt(rank ** skew) + 1 for rank in range(1, count + 1)]
    largest = limit if full else min(limit, max(-(-total // count), total * weights[0] // sum(weights)))
    least = 1 if total - largest >= count - 1 else 0
    counts, spare = [largest] + [least] * (count - 1), total - largest - least * (count - 1)
    while spare > 0:
        free = [i for i in range(1, count) if counts[i] < largest] or [i for i in range(1, count) if counts[i] < limit]
        mass, remaining = sum([weights[i] for i in free]), spare
        for i in free:
            more = min(limit - counts[i], max(1, remaining * weights[i] // mass), spare)
            counts[i] = counts[i] + more
            spare = spare - more
    return np.array(counts)


def centred(rng, dims, spread, most, cuts=(), kind=jnp.bfloat16):
    values = spread * jax.random.normal(rng, dims, jnp.float32)
    if cuts:
        values = values * shard_levels(rng, dims, cuts, -0.22, 0.18)
    return jnp.clip(values, -most, most).astype(kind)


def setup_inputs(seed: int = 0) -> dict:
    streams_of = jax.random.split(jax.random.key(seed), 18)
    tokens = centred(streams_of[0], (MB, TOKENS, D), 1.0, 6.0, ((1, 32),))
    cotangent = centred(streams_of[1], (MB, TOKENS, D), 1.0, 6.0, ((1, 32),))
    lengths = jax.vmap(lambda own: uneven_parts(own, NSEQ, TOKENS, LMAX, 1))(jax.random.split(streams_of[2], MB)).reshape((MB, NSEQ)).astype(jnp.int32)
    dealing = jax.vmap(lambda own: jax.random.permutation(own, TOKENS))(jax.random.split(streams_of[3], MB)).reshape((MB, TOKENS)).astype(jnp.int32)
    routes_keys = jax.random.split(jax.random.fold_in(streams_of[4], 1), MB * TOKENS // TOK)
    routes_turns = jax.random.permutation(jax.random.fold_in(streams_of[4], 3), MB * TOKENS // TOK)
    routes = jax.vmap(lambda own, number: deal_out(jax.random.fold_in(streams_of[4], 2), own, number, TOK, EXPERTS, TOPK, CAP, 1))(routes_keys, routes_turns).reshape((MB, TOKENS, TOPK))
    gate_weights = jnp.clip(jnp.exp(math.log(0.5) - 1.609438 * jax.random.uniform(streams_of[5], (MB, TOKENS, TOPK), jnp.float32) ** shard_levels(streams_of[5], (MB, TOKENS, TOPK), ((1, 8),), -0.2, 0.2)), 0.1, 0.5)
    attention_gain = jnp.clip(1.0 + 0.1 * jax.random.normal(streams_of[6], (D,), jnp.float32), 0.5, 1.5)
    mixture_gain = jnp.clip(1.0 + 0.1 * jax.random.normal(streams_of[7], (D,), jnp.float32), 0.5, 1.5)
    query_gain = jnp.clip(1.0 + 0.1 * jax.random.normal(streams_of[8], (HEAD,), jnp.float32), 0.5, 1.5)
    key_gain = jnp.clip(1.0 + 0.1 * jax.random.normal(streams_of[9], (HEAD,), jnp.float32), 0.5, 1.5)
    query_weight = centred(streams_of[10], (D, HEADS * HEAD), D ** -0.5, 0.125, ((0, 8), (1, 4)))
    key_weight = centred(streams_of[11], (D, HEADS * HEAD), D ** -0.5, 0.125, ((0, 8), (1, 4)))
    value_weight = centred(streams_of[12], (D, HEADS * HEAD), D ** -0.5, 0.125, ((0, 8), (1, 4)))
    out_weight = centred(streams_of[13], (D, HEADS * HEAD), (max(4, HEADS * HEAD // 256)) ** -0.5, 2.0, ((0, 8), (1, 4)))
    gate_weight = centred(streams_of[14], (EXPERTS, D, FF), D ** -0.5, 0.125, ((0, 8), (2, 4)))
    up_weight = centred(streams_of[15], (EXPERTS, D, FF), D ** -0.5, 0.125, ((0, 8), (2, 4)))
    down_weight = centred(streams_of[16], (EXPERTS, FF, D), (FF // 4) ** -0.5, 0.375, ((0, 8), (1, 4)))
    return {"tokens": tokens, "cotangent": cotangent, "lengths": lengths, "dealing": dealing, "routes": routes, "gate_weights": gate_weights, "attention_gain": attention_gain, "mixture_gain": mixture_gain, "query_gain": query_gain, "key_gain": key_gain, "query_weight": query_weight, "key_weight": key_weight, "value_weight": value_weight, "out_weight": out_weight, "gate_weight": gate_weight, "up_weight": up_weight, "down_weight": down_weight}


norm_epsilon = 1e-05
head_epsilon = 1e-06
rope_base = 50000.0
mask_value = -1e+30
highest = lax.Precision.HIGHEST

@jax.custom_vjp
def low(v):
    return lax.optimization_barrier(v.astype(jnp.bfloat16)).astype(jnp.float32)

@jax.custom_vjp
def low_back(v):
    return v

def low_keep(v):
    return (low(v), None)

def low_pass(kept, grad):
    return (grad,)

def back_keep(v):
    return (v, None)

def back_low(kept, grad):
    return (low(grad),)
low.defvjp(low_keep, low_pass)
low_back.defvjp(back_keep, back_low)

def rms_norm(value, gain):
    return value * lax.rsqrt(lax.optimization_barrier(jnp.mean(value * value, axis=-1, keepdims=True)) + norm_epsilon) * gain

def head_norm(value, gain):
    return value * lax.rsqrt(lax.optimization_barrier(jnp.mean(value * value, axis=-1, keepdims=True)) + head_epsilon) * gain

def rotate(value, cosine, sine):
    half = value.shape[-1] // 2
    first = value[..., :half]
    second = value[..., half:]
    return jnp.concatenate([first * cosine - second * sine, second * cosine + first * sine], axis=-1)

def angles(position):
    half = HEAD // 2
    rates = rope_base ** (-2.0 * jnp.arange(half, dtype=jnp.float32) / HEAD)
    theta = position.astype(jnp.float32)[:, None] * rates[None, :]
    return (jnp.cos(theta)[:, None, :], jnp.sin(theta)[:, None, :])

def layout(lengths_row, dealt):
    ends = jnp.cumsum(lengths_row).astype(jnp.int32)
    starts = (ends - lengths_row).astype(jnp.int32)
    segment = lax.optimization_barrier(jnp.sum((dealt[:, None] >= ends[None, :]).astype(jnp.int32), axis=1)).astype(jnp.int32)
    chosen = segment[:, None] == jnp.arange(lengths_row.shape[0], dtype=jnp.int32)[None, :]
    position = dealt - lax.optimization_barrier(jnp.sum(jnp.where(chosen, starts[None, :], 0), axis=1)).astype(jnp.int32)
    return (segment, position.astype(jnp.int32))

def slot_rows(route_rows):
    flat = route_rows.reshape(-1).astype(jnp.int32)
    onehot = (flat[:, None] == jnp.arange(EXPERTS, dtype=jnp.int32)[None, :]).astype(jnp.int32)
    before = jnp.cumsum(onehot, axis=0).astype(jnp.int32) - onehot
    slot = lax.optimization_barrier(jnp.sum(before * onehot, axis=1)).astype(jnp.int32)
    return (flat * CAP + slot).astype(jnp.int32)

def forward(source, attention_gain, mixture_gain, query_gain, key_gain, query_weight, key_weight, value_weight, out_weight, gate_weight, up_weight, down_weight, segment, cosine, sine, owner, target, gates):
    count = source.shape[0]
    normed_one = low(rms_norm(source, attention_gain))

    def project(matrix):
        return jnp.dot(normed_one, matrix, precision=highest).reshape(count, HEADS, HEAD)
    query_proj = low_back(project(query_weight))
    key_proj = low_back(project(key_weight))
    value_low = low(low_back(project(value_weight)))
    query_rot = low(rotate(head_norm(query_proj, query_gain), cosine, sine))
    key_rot = low(rotate(head_norm(key_proj, key_gain), cosine, sine))
    block = math.gcd(count, 512)
    scale = HEAD ** (-0.5)

    def attend(start):
        query_block = lax.dynamic_slice_in_dim(query_rot, start, block, 0)
        segment_block = lax.dynamic_slice_in_dim(segment, start, block, 0)
        raw = low_back(jnp.einsum('qhd,khd->hqk', query_block, key_rot, precision=highest))
        score = jnp.where((segment_block[:, None] == segment[None, :])[None], raw * scale, mask_value)
        top = lax.optimization_barrier(jnp.max(score, axis=-1, keepdims=True))
        powered = jnp.exp(score - top)
        share = powered / lax.optimization_barrier(jnp.sum(powered, axis=-1, keepdims=True))
        return jnp.einsum('hqk,khd->qhd', low(share), value_low, precision=highest)
    starts = jnp.arange(count // block, dtype=jnp.int32) * block
    mixed = lax.map(jax.checkpoint(attend), starts).reshape(count, HEADS * HEAD)
    mixed_low = low(low_back(mixed))
    state = source + low_back(jnp.dot(mixed_low, out_weight.T, precision=highest))
    normed_two = low(rms_norm(state, mixture_gain))
    padded = jnp.concatenate([jnp.zeros((1, D), jnp.float32), normed_two], axis=0)
    buffer = padded[owner].reshape(N_FSDP, EXPERTS, CAP, D)
    span = FF // N_TP
    total = jnp.zeros(buffer.shape, jnp.float32)
    for part in range(N_TP):
        inputs = low_back(buffer)
        gate_part = gate_weight[:, :, part * span:(part + 1) * span]
        up_part = up_weight[:, :, part * span:(part + 1) * span]
        down_part = down_weight[:, part * span:(part + 1) * span, :]
        gate_act = low_back(jnp.einsum('gecd,edf->gecf', inputs, gate_part, precision=highest))
        up_act = low_back(jnp.einsum('gecd,edf->gecf', inputs, up_part, precision=highest))
        hidden = low(jax.nn.silu(gate_act) * up_act)
        total = total + low(low_back(jnp.einsum('gecf,efd->gecd', hidden, down_part, precision=highest)))
    picked = total.reshape(-1, D)[target].reshape(count, TOPK, D)
    return state + lax.optimization_barrier(jnp.sum(gates[:, :, None] * picked, axis=1))

def reference(tokens, cotangent, lengths, dealing, routes, gate_weights, attention_gain, mixture_gain, query_gain, key_gain, query_weight, key_weight, value_weight, out_weight, gate_weight, up_weight, down_weight):
    params = tuple((item.astype(jnp.float32) for item in (attention_gain, mixture_gain, query_gain, key_gain, query_weight, key_weight, value_weight, out_weight, gate_weight, up_weight, down_weight)))
    grads = tuple((jnp.zeros(item.shape, jnp.float32) for item in params))
    outputs = []
    input_grads = []
    count = tokens.shape[1]
    for micro_step in range(MB):
        segment, position = layout(lengths[micro_step].astype(jnp.int32), dealing[micro_step].astype(jnp.int32))
        cosine, sine = angles(position)
        groups = routes[micro_step].reshape(N_FSDP, count // N_FSDP, TOPK)
        offsets = jnp.arange(N_FSDP, dtype=jnp.int32)[:, None] * (EXPERTS * CAP)
        target = (jax.vmap(slot_rows)(groups) + offsets).reshape(-1).astype(jnp.int32)
        entries = (jnp.arange(count * TOPK, dtype=jnp.int32) // TOPK + 1).astype(jnp.int32)
        owner = jnp.zeros((N_FSDP * EXPERTS * CAP,), jnp.int32).at[target].set(entries)
        gates = gate_weights[micro_step].astype(jnp.float32)

        def layer(source, *weights):
            return forward(source, *weights, segment, cosine, sine, owner, target, gates)
        result, pull = jax.vjp(layer, tokens[micro_step].astype(jnp.float32), *params)
        pulled = pull(cotangent[micro_step].astype(jnp.float32))
        outputs.append(result.astype(jnp.bfloat16))
        input_grads.append(pulled[0])
        grads = tuple((old + new for old, new in zip(grads, pulled[1:])))
    return (jnp.stack(outputs), jnp.stack(input_grads), grads[0], grads[1], grads[2], grads[3], grads[4], grads[5], grads[6], grads[7], grads[8], grads[9], grads[10])
```

```python
import math

import jax
import jax.numpy as jnp
from jax import lax
from jax.experimental import pallas as pl
from jax.experimental.pallas import tpu as pltpu
from jax.sharding import PartitionSpec as P

HEAD = 128
EXPERTS = 64
TOPK = 8
CAP = 48

norm_epsilon = 1e-05
head_epsilon = 1e-06
rope_base = 50000.0
mask_value = -1e30
scale = HEAD ** (-0.5)
bf16 = jnp.bfloat16
f32 = jnp.float32


def rms_norm(value, gain):
    return value * lax.rsqrt(jnp.mean(value * value, axis=-1, keepdims=True) + norm_epsilon) * gain


def head_norm(value, gain):
    return value * lax.rsqrt(jnp.mean(value * value, axis=-1, keepdims=True) + head_epsilon) * gain


def rotate(value, cosine, sine):
    half = value.shape[-1] // 2
    first = value[..., :half]
    second = value[..., half:]
    return jnp.concatenate(
        [first * cosine - second * sine, second * cosine + first * sine], axis=-1
    )


def angles(position):
    half = HEAD // 2
    rates = rope_base ** (-2.0 * jnp.arange(half, dtype=f32) / HEAD)
    theta = position.astype(f32)[:, None] * rates[None, :]
    return (jnp.cos(theta)[:, None, :], jnp.sin(theta)[:, None, :])


def layout(lengths_row, dealt):
    ends = jnp.cumsum(lengths_row)
    starts = ends - lengths_row
    segment = jnp.sum((dealt[:, None] >= ends[None, :]).astype(jnp.int32), axis=1)
    chosen = segment[:, None] == jnp.arange(lengths_row.shape[0], dtype=jnp.int32)[None, :]
    position = dealt - jnp.sum(jnp.where(chosen, starts[None, :], 0), axis=1)
    return (segment, position)


def relative(value, axis, own):
    size = value.shape[axis]
    bit = 1
    while bit < size:
        shape = value.shape[:axis] + (size // (2 * bit), 2, bit) + value.shape[axis + 1 :]
        split = value.reshape(shape)
        flipped = jnp.flip(split, axis + 1)
        value = jnp.where((own & bit) != 0, flipped, split).reshape(value.shape)
        bit *= 2
    return value


def swap(value, axis_name, size, distance):
    return lax.ppermute(value, axis_name, [(i, i ^ distance) for i in range(size)])


def rounded_sum(*parts):
    total = parts[0].astype(f32)
    for part in parts[1:]:
        total = total + part.astype(f32)
    return total


class Exchange:
    def __init__(self, n_fsdp, n_tp):
        self.n_fsdp = n_fsdp
        self.n_tp = n_tp

    def f(self, value, distance):
        return swap(value, "fsdp", self.n_fsdp, distance)

    def t(self, value, distance):
        return swap(value, "tp", self.n_tp, distance)

    def gather_tp(self, rows, axis):
        parts = [rows] + [self.t(rows, d) for d in range(1, self.n_tp)]
        return jnp.concatenate(parts, axis=axis)

    def scatter_tp(self, blocks):
        low = blocks.astype(bf16)
        return rounded_sum(blocks[0], *[self.t(low[d], d) for d in range(1, self.n_tp)])

    def gather_fsdp(self, rows, axis):
        if self.n_fsdp != 8:
            return [rows] + [self.f(rows, d) for d in range(1, self.n_fsdp)]
        half = rows.shape[axis] // 2
        from_x = self.f(rows, 2)
        from_y = self.f(rows, 4)
        from_core = self.f(rows, 1)
        low = self.f(lax.slice_in_dim(from_y, 0, half, axis=axis), 2)
        high = self.f(lax.slice_in_dim(from_x, half, 2 * half, axis=axis), 4)
        far = jnp.concatenate([low, high], axis=axis)
        return [
            rows,
            from_core,
            from_x,
            self.f(from_x, 1),
            from_y,
            self.f(from_y, 1),
            far,
            self.f(far, 1),
        ]

    def scatter_fsdp(self, even, odd):
        if self.n_fsdp != 8:
            parts = [even[0]]
            for d in range(1, self.n_fsdp):
                source = odd if d % 2 else even
                parts.append(self.f(source[d // 2], d))
            return parts
        both = rounded_sum(even, self.f(odd, 1)).astype(bf16)
        half = both.shape[1] // 2
        low = self.f(both[3, :half], 2)
        high = self.f(both[3, half:], 4)
        to_y = jnp.concatenate(
            [rounded_sum(both[2, :half], low).astype(bf16), both[2, half:]], axis=0
        )
        to_x = jnp.concatenate(
            [both[1, :half], rounded_sum(both[1, half:], high).astype(bf16)], axis=0
        )
        return [both[0], self.f(to_x, 2), self.f(to_y, 4)]


def one_hot(slot):
    experts, rows = slot.shape
    places = lax.broadcasted_iota(jnp.int32, (CAP, rows), 0)
    return jnp.concatenate(
        [
            jnp.where(slot[e : e + 1, :] == places, 1.0, 0.0).astype(bf16)
            for e in range(experts)
        ],
        axis=0,
    )


def dispatch(parts, micro_step, slot, gates):
    groups, experts, rows = slot.shape
    width = parts[0].shape[-1]
    stacked = parts[0].ndim == 3
    scaled = gates is not None

    def kernel(*refs):
        slot_ref = refs[0]
        refs = refs[1:]
        if scaled:
            gate_ref = refs[0]
            refs = refs[1:]
        sources = refs[:groups]
        refs = refs[groups:]
        out_ref = refs[0]
        refs = refs[1:]
        if scaled:
            slot_gate_ref = refs[0]
            refs = refs[1:]
        buffer, semaphore = refs
        step = pl.program_id(0)

        def copy(j, place):
            source = sources[j].at[micro_step] if stacked else sources[j]
            return pltpu.make_async_copy(source, buffer.at[place], semaphore.at[place])

        @pl.when(step == 0)
        def _():
            copy(0, 0).start()

        for j in range(groups):
            @pl.when(step == j)
            def _():
                if j + 1 < groups:
                    copy(j + 1, (j + 1) % 2).start()
                copy(j, j % 2).wait()

        chosen = one_hot(slot_ref[0])
        taken = jnp.dot(chosen, buffer[step % 2], preferred_element_type=f32)
        if scaled:
            wide = jnp.concatenate(
                [jnp.broadcast_to(gate_ref[0, e : e + 1, :], (CAP, rows)) for e in range(experts)],
                axis=0,
            )
            level = jnp.sum(jnp.where(chosen > 0, wide, 0.0), axis=1, keepdims=True)
            taken = taken * level
            slot_gate_ref[...] = jnp.broadcast_to(level, (experts * CAP, 128)).reshape(
                experts, 1, CAP, 128
            )
        out_ref[...] = taken.astype(bf16).reshape(experts, 1, CAP, width)

    small = pl.BlockSpec((1, experts, rows), lambda g: (g, 0, 0))
    out_shape = [jax.ShapeDtypeStruct((experts, groups, CAP, width), bf16)]
    out_specs = [pl.BlockSpec((experts, 1, CAP, width), lambda g: (0, g, 0, 0))]
    if scaled:
        out_shape.append(jax.ShapeDtypeStruct((experts, groups, CAP, 128), f32))
        out_specs.append(pl.BlockSpec((experts, 1, CAP, 128), lambda g: (0, g, 0, 0)))
    operands = [slot] + ([gates] if scaled else []) + list(parts)
    result = pl.pallas_call(
        kernel,
        grid=(groups,),
        in_specs=[small] * (2 if scaled else 1) + [pl.BlockSpec(memory_space=pl.ANY)] * groups,
        out_specs=out_specs,
        out_shape=out_shape,
        scratch_shapes=[pltpu.VMEM((2, rows, width), bf16), pltpu.SemaphoreType.DMA((2,))],
        name="dispatch_grad" if scaled else "dispatch",
    )(*operands)
    return result if scaled else result[0]


def combine(values, slot):
    experts, groups, _, width = values.shape
    rows = slot.shape[-1]

    def kernel(slot_ref, value_ref, even_ref, odd_ref):
        chosen = one_hot(slot_ref[0])
        summed = lax.dot_general(
            chosen,
            value_ref[...].reshape(experts * CAP, width),
            (((0,), (0,)), ((), ())),
            preferred_element_type=f32,
        ).astype(bf16)
        step = pl.program_id(0)

        @pl.when(step % 2 == 0)
        def _():
            even_ref[0] = summed

        @pl.when(step % 2 == 1)
        def _():
            odd_ref[0] = summed

    return pl.pallas_call(
        kernel,
        grid=(groups,),
        in_specs=[
            pl.BlockSpec((1, experts, rows), lambda g: (g, 0, 0)),
            pl.BlockSpec((experts, 1, CAP, width), lambda g: (0, g, 0, 0)),
        ],
        out_specs=[pl.BlockSpec((1, rows, width), lambda g: (g // 2, 0, 0))] * 2,
        out_shape=[jax.ShapeDtypeStruct((groups // 2, rows, width), bf16)] * 2,
        name="combine",
    )(slot, values)


def experts_step(arrived, grad_arrived, slot_gate, gate_weight, up_weight, down_weight):
    experts, groups, _, width = arrived.shape
    hidden = gate_weight.shape[2]
    chunk = math.gcd(groups, 8)
    rows = chunk * CAP

    def kernel(x_ref, g_ref, level_ref, wg_ref, wu_ref, wd_ref, y_ref, gx_ref, h_ref, dg_ref, du_ref):
        x = x_ref[...].reshape(rows, width)
        gate_act = jnp.dot(x, wg_ref[0], preferred_element_type=f32)
        up_act = jnp.dot(x, wu_ref[0], preferred_element_type=f32)
        sig = 1.0 / (1.0 + jnp.exp(-gate_act))
        silu = gate_act * sig
        h = (silu * up_act).astype(bf16)
        h_ref[...] = h.reshape(h_ref.shape)
        y = jnp.dot(h, wd_ref[0], preferred_element_type=f32)
        level = level_ref[...].reshape(rows, 128)[:, :1]
        y_ref[...] = (y * level).astype(bf16).reshape(y_ref.shape)
        g = g_ref[...].reshape(rows, width)
        nt = (((1,), (1,)), ((), ()))
        grad_h = lax.dot_general(g, wd_ref[0], nt, preferred_element_type=f32)
        dg = (grad_h * up_act * (sig * (1.0 + gate_act * (1.0 - sig)))).astype(bf16)
        du = (grad_h * silu).astype(bf16)
        dg_ref[...] = dg.reshape(dg_ref.shape)
        du_ref[...] = du.reshape(du_ref.shape)
        gx = lax.dot_general(dg, wg_ref[0], nt, preferred_element_type=f32)
        gx = gx + lax.dot_general(du, wu_ref[0], nt, preferred_element_type=f32)
        gx_ref[...] = gx.astype(bf16).reshape(gx_ref.shape)

    wide = pl.BlockSpec((1, chunk, CAP, width), lambda e, c: (e, c, 0, 0))
    narrow = pl.BlockSpec((1, chunk, CAP, hidden), lambda e, c: (e, c, 0, 0))
    level = pl.BlockSpec((1, chunk, CAP, 128), lambda e, c: (e, c, 0, 0))
    column = pl.BlockSpec((1, width, hidden), lambda e, c: (e, 0, 0))
    line = pl.BlockSpec((1, hidden, width), lambda e, c: (e, 0, 0))
    small = jax.ShapeDtypeStruct((experts, groups, CAP, hidden), bf16)
    big = jax.ShapeDtypeStruct(arrived.shape, bf16)
    return pl.pallas_call(
        kernel,
        grid=(experts, groups // chunk),
        in_specs=[wide, wide, level, column, column, line],
        out_specs=[wide, wide, narrow, narrow, narrow],
        out_shape=[big, big, small, small, small],
        name="experts",
    )(arrived, grad_arrived, slot_gate, gate_weight, up_weight, down_weight)


def expert_weight_grads(saved):
    experts, groups, _, width = saved[0][0].shape
    hidden = saved[0][2].shape[-1]
    chunk = math.gcd(groups, 8)
    rows = chunk * CAP
    count = len(saved)

    def kernel(*refs):
        out_refs = refs[5 * count :]
        tn = (((0,), (0,)), ((), ()))

        def total(left, right, left_width, right_width):
            result = None
            for m in range(count):
                a = refs[5 * m + left][...].reshape(rows, left_width)
                b = refs[5 * m + right][...].reshape(rows, right_width)
                part = lax.dot_general(a, b, tn, preferred_element_type=f32)
                result = part if result is None else result + part
            return result

        values = (
            total(0, 3, width, hidden),
            total(0, 4, width, hidden),
            total(2, 1, hidden, width),
        )
        if groups == chunk:
            for ref, value in zip(out_refs, values):
                ref[0] = value
        else:
            first = pl.program_id(1) == 0

            @pl.when(first)
            def _():
                for ref, value in zip(out_refs, values):
                    ref[0] = value

            @pl.when(jnp.logical_not(first))
            def _():
                for ref, value in zip(out_refs, values):
                    ref[0] = ref[0] + value

    wide = pl.BlockSpec((1, chunk, CAP, width), lambda e, c: (e, c, 0, 0))
    narrow = pl.BlockSpec((1, chunk, CAP, hidden), lambda e, c: (e, c, 0, 0))
    column = pl.BlockSpec((1, width, hidden), lambda e, c: (e, 0, 0))
    line = pl.BlockSpec((1, hidden, width), lambda e, c: (e, 0, 0))
    return pl.pallas_call(
        kernel,
        grid=(experts, groups // chunk),
        in_specs=[wide, wide, narrow, narrow, narrow] * count,
        out_specs=[column, column, line],
        out_shape=[
            jax.ShapeDtypeStruct((experts, width, hidden), f32),
            jax.ShapeDtypeStruct((experts, width, hidden), f32),
            jax.ShapeDtypeStruct((experts, hidden, width), f32),
        ],
        name="expert_weight_grads",
    )(*[item for entry in saved for item in entry])


NT = (((1,), (1,)), ((), ()))
TN = (((0,), (0,)), ((), ()))


def masked_scores(query, keys, query_segment, key_segment):
    raw = lax.dot_general(query, keys, NT, preferred_element_type=f32)
    return jnp.where(query_segment == key_segment, raw * scale, mask_value)


def attend_forward(own, other, query_segment, key_segment):
    queries = own.shape[0]
    others = other.shape[0]
    block = math.gcd(queries, 256)

    def kernel(query_ref, own_ref, other_ref, qs_ref, ks_ref, out_ref, log_ref):
        query = query_ref[...]
        segment = qs_ref[...]
        first = masked_scores(query, own_ref[:, HEAD : 2 * HEAD], segment, ks_ref[:, :queries])
        second = masked_scores(query, other_ref[:, :HEAD], segment, ks_ref[:, queries:])
        top = jnp.maximum(
            jnp.max(first, axis=1, keepdims=True), jnp.max(second, axis=1, keepdims=True)
        )
        first = jnp.exp(first - top)
        second = jnp.exp(second - top)
        total = jnp.sum(first, axis=1, keepdims=True) + jnp.sum(second, axis=1, keepdims=True)
        inverse = 1.0 / total
        mixed = jnp.dot(
            (first * inverse).astype(bf16), own_ref[:, 2 * HEAD :], preferred_element_type=f32
        )
        mixed = mixed + jnp.dot(
            (second * inverse).astype(bf16), other_ref[:, HEAD:], preferred_element_type=f32
        )
        out_ref[...] = mixed.astype(bf16)
        log_ref[...] = jnp.broadcast_to(top + jnp.log(total), log_ref.shape)

    return pl.pallas_call(
        kernel,
        grid=(queries // block,),
        in_specs=[
            pl.BlockSpec((block, HEAD), lambda i: (i, 0)),
            pl.BlockSpec(own.shape, lambda i: (0, 0)),
            pl.BlockSpec(other.shape, lambda i: (0, 0)),
            pl.BlockSpec((block, 1), lambda i: (i, 0)),
            pl.BlockSpec((1, queries + others), lambda i: (0, 0)),
        ],
        out_specs=[
            pl.BlockSpec((block, HEAD), lambda i: (i, 0)),
            pl.BlockSpec((block, 128), lambda i: (i, 0)),
        ],
        out_shape=[
            jax.ShapeDtypeStruct((queries, HEAD), bf16),
            jax.ShapeDtypeStruct((queries, 128), f32),
        ],
        name="attend_forward",
    )(own, own, other, query_segment, key_segment)


def attend_backward(own, other, grad_out, log_total, query_segment, key_segment):
    queries = own.shape[0]
    others = other.shape[0]
    block = math.gcd(queries, 256)

    def kernel(
        query_ref, own_ref, other_ref, grad_ref, log_ref, qs_ref, ks_ref, dq_ref, own_out, other_out
    ):
        query = query_ref[...]
        grad = grad_ref[...]
        segment = qs_ref[...]
        log_value = log_ref[:, :1]
        k1 = own_ref[:, HEAD : 2 * HEAD]
        v1 = own_ref[:, 2 * HEAD :]
        k2 = other_ref[:, :HEAD]
        v2 = other_ref[:, HEAD:]
        p1 = jnp.exp(masked_scores(query, k1, segment, ks_ref[:, :queries]) - log_value)
        p2 = jnp.exp(masked_scores(query, k2, segment, ks_ref[:, queries:]) - log_value)
        g1 = lax.dot_general(grad, v1, NT, preferred_element_type=f32)
        g2 = lax.dot_general(grad, v2, NT, preferred_element_type=f32)
        delta = jnp.sum(p1 * g1, axis=1, keepdims=True) + jnp.sum(p2 * g2, axis=1, keepdims=True)
        s1 = (p1 * (g1 - delta) * scale).astype(bf16)
        s2 = (p2 * (g2 - delta) * scale).astype(bf16)
        dq = jnp.dot(s1, k1, preferred_element_type=f32)
        dq = dq + jnp.dot(s2, k2, preferred_element_type=f32)
        dq_ref[...] = dq.astype(bf16)

        @pl.when(pl.program_id(0) == 0)
        def _():
            own_out[...] = jnp.zeros_like(own_out)
            other_out[...] = jnp.zeros_like(other_out)

        own_out[:, :HEAD] += lax.dot_general(s1, query, TN, preferred_element_type=f32)
        own_out[:, HEAD:] += lax.dot_general(p1.astype(bf16), grad, TN, preferred_element_type=f32)
        other_out[:, :HEAD] += lax.dot_general(s2, query, TN, preferred_element_type=f32)
        other_out[:, HEAD:] += lax.dot_general(p2.astype(bf16), grad, TN, preferred_element_type=f32)

    rows = pl.BlockSpec((block, HEAD), lambda i: (i, 0))
    return pl.pallas_call(
        kernel,
        grid=(queries // block,),
        in_specs=[
            rows,
            pl.BlockSpec(own.shape, lambda i: (0, 0)),
            pl.BlockSpec(other.shape, lambda i: (0, 0)),
            rows,
            pl.BlockSpec((block, 128), lambda i: (i, 0)),
            pl.BlockSpec((block, 1), lambda i: (i, 0)),
            pl.BlockSpec((1, queries + others), lambda i: (0, 0)),
        ],
        out_specs=[
            rows,
            pl.BlockSpec((queries, 2 * HEAD), lambda i: (0, 0)),
            pl.BlockSpec((others, 2 * HEAD), lambda i: (0, 0)),
        ],
        out_shape=[
            jax.ShapeDtypeStruct((queries, HEAD), bf16),
            jax.ShapeDtypeStruct((queries, 2 * HEAD), f32),
            jax.ShapeDtypeStruct((others, 2 * HEAD), f32),
        ],
        name="attend_backward",
    )(own, own, other, grad_out, log_total, query_segment, key_segment)


def make_body(n_fsdp, n_tp):
    move = Exchange(n_fsdp, n_tp)

    def body(
        tokens,
        cotangent,
        lengths,
        dealing,
        routes,
        gate_weights,
        attention_gain,
        mixture_gain,
        query_gain,
        key_gain,
        query_weight,
        key_weight,
        value_weight,
        out_weight,
        gate_weight,
        up_weight,
        down_weight,
    ):
        micro, rows, width = tokens.shape
        group = routes.shape[1]
        experts = gate_weight.shape[0]
        f_own = lax.axis_index("fsdp")
        t_own = lax.axis_index("tp")
        inner = query_weight.shape[1]
        heads = inner // HEAD
        sharers = n_fsdp // heads
        head_own = f_own // sharers

        packed = jnp.concatenate([query_weight, key_weight, value_weight], axis=1)
        packed_full = lax.all_gather(packed, "fsdp", axis=0, tiled=True)
        out_full = lax.all_gather(out_weight, "fsdp", axis=0, tiled=True)

        source = tokens.astype(f32)
        normed_one = move.gather_tp(rms_norm(source, attention_gain).astype(bf16), 1)

        ids = jnp.arange(EXPERTS, dtype=jnp.int32)[None, :, None]
        dense = jnp.zeros((micro, EXPERTS, group), f32)
        for choose in range(TOPK):
            hit = routes[:, None, :, choose] == ids
            dense = dense + jnp.where(hit, gate_weights[:, None, :, choose], 0.0)
        every = lax.all_gather(dense, "fsdp", axis=0, tiled=False)
        mine = lax.dynamic_slice_in_dim(every, f_own * experts, experts, 2)
        mine = relative(mine, 0, f_own)
        mine = relative(
            mine.reshape(n_fsdp, micro, experts, n_tp, rows), 3, t_own
        ).reshape(n_fsdp, micro, experts, group)
        mine = jnp.transpose(mine, (1, 0, 2, 3))
        named = mine > 0.0
        earlier = jnp.triu(jnp.ones((group, group), bf16), 1)
        before = jnp.einsum(
            "mgei,ij->mgej", named.astype(bf16), earlier, preferred_element_type=f32
        )
        slots = jnp.where(named, before.astype(jnp.int32), -1)

        grad_rows = cotangent
        grad_parts = move.gather_fsdp(move.gather_tp(grad_rows, 1), 1)

        dealt = relative(dealing.reshape(micro, n_fsdp, n_tp, rows), 1, f_own)
        dealt = relative(dealt, 2, t_own).reshape(micro, n_fsdp, group)
        order = []
        for lead in range(sharers):
            order += [lead + sharers * p for p in range(heads)]

        def exchange_heads(blocks):
            parts = [blocks[0]] + [
                move.f(blocks[d], d * sharers) for d in range(1, heads)
            ]
            return jnp.stack(parts)

        outputs = []
        input_grads = []
        saved = []
        out_acc = None
        qkv_acc = None
        attention_acc = 0.0
        mixture_acc = 0.0
        qgain_acc = 0.0
        kgain_acc = 0.0
        for m in range(micro):
            ordered = jnp.stack([dealt[m, d] for d in order])
            segment, _ = layout(lengths[m], ordered.reshape(-1))
            query_segment = segment[: heads * group].reshape(-1, 1)
            key_segment = segment.reshape(1, -1)
            _, position = layout(lengths[m], dealt[m, 0])
            cosine, sine = angles(position)

            def shape_heads(projected, gain):
                return rotate(head_norm(projected, gain), cosine, sine)

            attn_input = normed_one[m]
            projected = jnp.dot(attn_input, packed_full, preferred_element_type=f32)
            query_proj = projected[:, :inner].reshape(group, heads, HEAD)
            key_proj = projected[:, inner : 2 * inner].reshape(group, heads, HEAD)
            value_low = projected[:, 2 * inner :].astype(bf16).reshape(group, heads, HEAD)
            query_rot = shape_heads(query_proj, query_gain).astype(bf16)
            key_rot = shape_heads(key_proj, key_gain).astype(bf16)
            bundle = jnp.concatenate([query_rot, key_rot, value_low], axis=2)
            bundle = relative(jnp.transpose(bundle, (1, 0, 2)), 0, head_own)
            own = exchange_heads(bundle).reshape(heads * group, 3 * HEAD)
            own_pair = own[:, HEAD:]
            other = jnp.concatenate([move.f(own_pair, d) for d in range(1, sharers)], axis=0)
            mixed, log_total = attend_forward(own, other, query_segment, key_segment)
            back = relative(exchange_heads(mixed.reshape(heads, group, HEAD)), 0, head_own)
            mixed_low = jnp.transpose(back, (1, 0, 2)).reshape(group, inner)
            attn_part = lax.dot_general(mixed_low, out_full, NT, preferred_element_type=f32)
            state = source[m] + move.scatter_tp(attn_part.reshape(n_tp, rows, width))
            normed_two = rms_norm(state, mixture_gain).astype(bf16)
            row_parts = move.gather_fsdp(move.gather_tp(normed_two, 0), 0)
            slot = slots[m]
            grad_arrived, slot_gate = dispatch(grad_parts, m, slot, mine[m])
            arrived = dispatch(row_parts, 0, slot, None)
            expert_out, grad_out, hidden, grad_gate, grad_up = experts_step(
                arrived, grad_arrived, slot_gate, gate_weight, up_weight, down_weight
            )
            saved.append((arrived, grad_arrived, hidden, grad_gate, grad_up))

            def to_rows(values):
                parts = move.scatter_fsdp(*combine(values, slot))
                return move.scatter_tp(rounded_sum(*parts).reshape(n_tp, rows, width))

            grad_normed_two = to_rows(grad_out)
            outputs.append((state + to_rows(expert_out)).astype(bf16))
            _, pull_two = jax.vjp(rms_norm, state, mixture_gain)
            grad_from_norm, grad_mixture = pull_two(grad_normed_two)
            mixture_acc = mixture_acc + grad_mixture
            grad_state = grad_rows[m].astype(f32) + grad_from_norm
            grad_state_group = move.gather_tp(grad_state.astype(bf16), 0)
            out_part = lax.dot_general(grad_state_group, mixed_low, TN, preferred_element_type=f32)
            out_acc = out_part if out_acc is None else out_acc + out_part
            grad_mixed = jnp.dot(grad_state_group, out_full, preferred_element_type=f32)
            grad_mixed = jnp.transpose(
                grad_mixed.astype(bf16).reshape(group, heads, HEAD), (1, 0, 2)
            )
            grad_heads = exchange_heads(relative(grad_mixed, 0, head_own))
            grad_query, sums_own, sums_other = attend_backward(
                own,
                other,
                grad_heads.reshape(heads * group, HEAD),
                log_total,
                query_segment,
                key_segment,
            )
            sums_other = sums_other.reshape(sharers - 1, heads * group, 2 * HEAD)
            sums = rounded_sum(
                sums_own, *[move.f(sums_other[d - 1], d) for d in range(1, sharers)]
            ).astype(bf16)
            back = jnp.concatenate([grad_query, sums], axis=1).reshape(heads, group, 3 * HEAD)
            back = relative(exchange_heads(back), 0, head_own)
            back = jnp.transpose(back, (1, 0, 2)).astype(f32)
            _, pull_query = jax.vjp(shape_heads, query_proj, query_gain)
            grad_query_proj, grad_qgain = pull_query(back[:, :, :HEAD])
            _, pull_key = jax.vjp(shape_heads, key_proj, key_gain)
            grad_key_proj, grad_kgain = pull_key(back[:, :, HEAD : 2 * HEAD])
            qgain_acc = qgain_acc + grad_qgain
            kgain_acc = kgain_acc + grad_kgain
            grad_low = jnp.concatenate(
                [
                    grad_query_proj.reshape(group, inner).astype(bf16),
                    grad_key_proj.reshape(group, inner).astype(bf16),
                    back[:, :, 2 * HEAD :].reshape(group, inner).astype(bf16),
                ],
                axis=1,
            )
            qkv_part = lax.dot_general(attn_input, grad_low, TN, preferred_element_type=f32)
            qkv_acc = qkv_part if qkv_acc is None else qkv_acc + qkv_part
            grad_input_attn = lax.dot_general(
                grad_low, packed_full, NT, preferred_element_type=f32
            )
            grad_normed_one = move.scatter_tp(grad_input_attn.reshape(n_tp, rows, width))
            _, pull_one = jax.vjp(rms_norm, source[m], attention_gain)
            grad_source, grad_attention = pull_one(grad_normed_one)
            attention_acc = attention_acc + grad_attention
            input_grads.append(grad_state + grad_source)
        gate_grad, up_grad, down_grad = expert_weight_grads(saved)
        out_grad = lax.psum_scatter(
            out_acc.astype(bf16), "fsdp", scatter_dimension=0, tiled=True
        ).astype(f32)
        qkv_grad = lax.psum_scatter(
            qkv_acc.astype(bf16), "fsdp", scatter_dimension=0, tiled=True
        ).astype(f32)
        attention_grad, mixture_grad, qgain_grad, kgain_grad = lax.psum(
            (attention_acc, mixture_acc, qgain_acc, kgain_acc), ("fsdp", "tp")
        )
        return (
            jnp.stack(outputs),
            jnp.stack(input_grads),
            attention_grad,
            mixture_grad,
            qgain_grad,
            kgain_grad,
            qkv_grad[:, :inner],
            qkv_grad[:, inner : 2 * inner],
            qkv_grad[:, 2 * inner :],
            out_grad,
            gate_grad,
            up_grad,
            down_grad,
        )

    return body


def solution(mesh):
    weight = P("fsdp", "tp")
    column = P("fsdp", None, "tp")
    line = P("fsdp", "tp", None)
    spread = P(None, ("fsdp", "tp"), None)
    routed = P(None, "fsdp", None)
    in_specs = (
        (spread, spread, P(), P(), routed, routed)
        + (P(),) * 4
        + (weight,) * 4
        + (column, column, line)
    )
    out_specs = (spread, spread) + (P(),) * 4 + (weight,) * 4 + (column, column, line)
    body = make_body(mesh.shape["fsdp"], mesh.shape["tp"])
    return jax.shard_map(body, mesh=mesh, in_specs=in_specs, out_specs=out_specs, check_vma=False)
```

```python
import math

import jax
import jax.numpy as jnp
from jax import lax
from jax.experimental import pallas as pl
from jax.experimental.pallas import tpu as pltpu
from jax.sharding import PartitionSpec as P

HEAD = 128
EXPERTS = 64
TOPK = 8
CAP = 48

norm_epsilon = 1e-05
head_epsilon = 1e-06
rope_base = 50000.0
mask_value = -1e30
scale = HEAD ** (-0.5)
bf16 = jnp.bfloat16
f32 = jnp.float32


def rms_norm(value, gain):
    return value * lax.rsqrt(jnp.mean(value * value, axis=-1, keepdims=True) + norm_epsilon) * gain


def head_norm(value, gain):
    return value * lax.rsqrt(jnp.mean(value * value, axis=-1, keepdims=True) + head_epsilon) * gain


def rotate(value, cosine, sine):
    half = value.shape[-1] // 2
    first = value[..., :half]
    second = value[..., half:]
    return jnp.concatenate(
        [first * cosine - second * sine, second * cosine + first * sine], axis=-1
    )


def angles(position):
    half = HEAD // 2
    rates = rope_base ** (-2.0 * jnp.arange(half, dtype=f32) / HEAD)
    theta = position.astype(f32)[:, None] * rates[None, :]
    return (jnp.cos(theta)[:, None, :], jnp.sin(theta)[:, None, :])


def layout(lengths_row, dealt):
    ends = jnp.cumsum(lengths_row)
    starts = ends - lengths_row
    segment = jnp.sum((dealt[:, None] >= ends[None, :]).astype(jnp.int32), axis=1)
    chosen = segment[:, None] == jnp.arange(lengths_row.shape[0], dtype=jnp.int32)[None, :]
    position = dealt - jnp.sum(jnp.where(chosen, starts[None, :], 0), axis=1)
    return (segment, position)


def relative(value, axis, own):
    size = value.shape[axis]
    bit = 1
    while bit < size:
        shape = value.shape[:axis] + (size // (2 * bit), 2, bit) + value.shape[axis + 1 :]
        split = value.reshape(shape)
        flipped = jnp.flip(split, axis + 1)
        value = jnp.where((own & bit) != 0, flipped, split).reshape(value.shape)
        bit *= 2
    return value


def swap(value, axis_name, size, distance):
    return lax.ppermute(value, axis_name, [(i, i ^ distance) for i in range(size)])


def rounded_sum(*parts):
    total = parts[0].astype(f32)
    for part in parts[1:]:
        total = total + part.astype(f32)
    return total


def after(value, earlier):
    return lax.optimization_barrier((value, earlier))[0]


class Exchange:
    def __init__(self, n_fsdp, n_tp):
        self.n_fsdp = n_fsdp
        self.n_tp = n_tp

    def f(self, value, distance):
        return swap(value, "fsdp", self.n_fsdp, distance)

    def t(self, value, distance):
        return swap(value, "tp", self.n_tp, distance)

    def total(self, value):
        for size, step in ((self.n_tp, self.t), (self.n_fsdp, self.f)):
            distance = 1
            while distance < size:
                value = value + step(value, distance)
                distance *= 2
        return value

    def gather_tp(self, rows, axis):
        parts = [rows] + [self.t(rows, d) for d in range(1, self.n_tp)]
        return jnp.concatenate(parts, axis=axis)

    def scatter_tp(self, blocks):
        low = blocks.astype(bf16)
        return rounded_sum(blocks[0], *[self.t(low[d], d) for d in range(1, self.n_tp)])

    def gather_fsdp(self, rows, axis):
        if self.n_fsdp != 8:
            return [rows] + [self.f(rows, d) for d in range(1, self.n_fsdp)]
        half = rows.shape[axis] // 2
        from_x = self.f(rows, 2)
        from_y = self.f(rows, 4)
        from_core = self.f(rows, 1)
        low = self.f(lax.slice_in_dim(from_y, 0, half, axis=axis), 2)
        high = self.f(lax.slice_in_dim(from_x, half, 2 * half, axis=axis), 4)
        far = jnp.concatenate([low, high], axis=axis)
        return [
            rows,
            from_core,
            from_x,
            self.f(from_x, 1),
            from_y,
            self.f(from_y, 1),
            far,
            self.f(far, 1),
        ]

    def scatter_fsdp(self, even, odd):
        if self.n_fsdp != 8:
            parts = [even[0]]
            for d in range(1, self.n_fsdp):
                source = odd if d % 2 else even
                parts.append(self.f(source[d // 2], d))
            return parts
        both = rounded_sum(even, self.f(odd, 1)).astype(bf16)
        half = both.shape[1] // 2
        low = self.f(both[3, :half], 2)
        high = self.f(both[3, half:], 4)
        to_y = jnp.concatenate(
            [rounded_sum(both[2, :half], low).astype(bf16), both[2, half:]], axis=0
        )
        to_x = jnp.concatenate(
            [both[1, :half], rounded_sum(both[1, half:], high).astype(bf16)], axis=0
        )
        return [both[0], self.f(to_x, 2), self.f(to_y, 4)]


def one_hot(slot):
    experts, rows = slot.shape
    places = lax.broadcasted_iota(jnp.int32, (CAP, rows), 0)
    return jnp.concatenate(
        [
            jnp.where(slot[e : e + 1, :] == places, 1.0, 0.0).astype(bf16)
            for e in range(experts)
        ],
        axis=0,
    )


def dispatch(parts, micro_step, slot, gates):
    groups, experts, rows = slot.shape
    width = parts[0].shape[-1]
    stacked = parts[0].ndim == 3
    scaled = gates is not None

    def kernel(*refs):
        slot_ref = refs[0]
        refs = refs[1:]
        if scaled:
            gate_ref = refs[0]
            refs = refs[1:]
        sources = refs[:groups]
        refs = refs[groups:]
        out_ref = refs[0]
        refs = refs[1:]
        if scaled:
            slot_gate_ref = refs[0]
            refs = refs[1:]
        buffer, semaphore = refs
        step = pl.program_id(0)

        def copy(j, place):
            source = sources[j].at[micro_step] if stacked else sources[j]
            return pltpu.make_async_copy(source, buffer.at[place], semaphore.at[place])

        @pl.when(step == 0)
        def _():
            copy(0, 0).start()

        for j in range(groups):
            @pl.when(step == j)
            def _():
                if j + 1 < groups:
                    copy(j + 1, (j + 1) % 2).start()
                copy(j, j % 2).wait()

        chosen = one_hot(slot_ref[0])
        taken = jnp.dot(chosen, buffer[step % 2], preferred_element_type=f32)
        if scaled:
            wide = jnp.concatenate(
                [jnp.broadcast_to(gate_ref[0, e : e + 1, :], (CAP, rows)) for e in range(experts)],
                axis=0,
            )
            level = jnp.sum(jnp.where(chosen > 0, wide, 0.0), axis=1, keepdims=True)
            taken = taken * level
            slot_gate_ref[...] = jnp.broadcast_to(level, (experts * CAP, 128)).reshape(
                experts, 1, CAP, 128
            )
        out_ref[...] = taken.astype(bf16).reshape(experts, 1, CAP, width)

    small = pl.BlockSpec((1, experts, rows), lambda g: (g, 0, 0))
    out_shape = [jax.ShapeDtypeStruct((experts, groups, CAP, width), bf16)]
    out_specs = [pl.BlockSpec((experts, 1, CAP, width), lambda g: (0, g, 0, 0))]
    if scaled:
        out_shape.append(jax.ShapeDtypeStruct((experts, groups, CAP, 128), f32))
        out_specs.append(pl.BlockSpec((experts, 1, CAP, 128), lambda g: (0, g, 0, 0)))
    operands = [slot] + ([gates] if scaled else []) + list(parts)
    result = pl.pallas_call(
        kernel,
        grid=(groups,),
        in_specs=[small] * (2 if scaled else 1) + [pl.BlockSpec(memory_space=pl.ANY)] * groups,
        out_specs=out_specs,
        out_shape=out_shape,
        scratch_shapes=[pltpu.VMEM((2, rows, width), bf16), pltpu.SemaphoreType.DMA((2,))],
        name="dispatch_grad" if scaled else "dispatch",
    )(*operands)
    return result if scaled else result[0]


def combine(values, slot):
    experts, groups, _, width = values.shape
    rows = slot.shape[-1]

    def kernel(slot_ref, value_ref, even_ref, odd_ref):
        chosen = one_hot(slot_ref[0])
        summed = lax.dot_general(
            chosen,
            value_ref[...].reshape(experts * CAP, width),
            (((0,), (0,)), ((), ())),
            preferred_element_type=f32,
        ).astype(bf16)
        step = pl.program_id(0)

        @pl.when(step % 2 == 0)
        def _():
            even_ref[0] = summed

        @pl.when(step % 2 == 1)
        def _():
            odd_ref[0] = summed

    return pl.pallas_call(
        kernel,
        grid=(groups,),
        in_specs=[
            pl.BlockSpec((1, experts, rows), lambda g: (g, 0, 0)),
            pl.BlockSpec((experts, 1, CAP, width), lambda g: (0, g, 0, 0)),
        ],
        out_specs=[pl.BlockSpec((1, rows, width), lambda g: (g // 2, 0, 0))] * 2,
        out_shape=[jax.ShapeDtypeStruct((groups // 2, rows, width), bf16)] * 2,
        name="combine",
    )(slot, values)


def experts_step(arrived, grad_arrived, slot_gate, gate_weight, up_weight, down_weight):
    experts, groups, _, width = arrived.shape
    hidden = gate_weight.shape[2]
    chunk = math.gcd(groups, 8)
    rows = chunk * CAP

    def kernel(x_ref, g_ref, level_ref, wg_ref, wu_ref, wd_ref, y_ref, gx_ref, h_ref, dg_ref, du_ref):
        x = x_ref[...].reshape(rows, width)
        gate_act = jnp.dot(x, wg_ref[0], preferred_element_type=f32)
        up_act = jnp.dot(x, wu_ref[0], preferred_element_type=f32)
        sig = 1.0 / (1.0 + jnp.exp(-gate_act))
        silu = gate_act * sig
        h = (silu * up_act).astype(bf16)
        h_ref[...] = h.reshape(h_ref.shape)
        y = jnp.dot(h, wd_ref[0], preferred_element_type=f32)
        level = level_ref[...].reshape(rows, 128)[:, :1]
        y_ref[...] = (y * level).astype(bf16).reshape(y_ref.shape)
        g = g_ref[...].reshape(rows, width)
        nt = (((1,), (1,)), ((), ()))
        grad_h = lax.dot_general(g, wd_ref[0], nt, preferred_element_type=f32)
        dg = (grad_h * up_act * (sig * (1.0 + gate_act * (1.0 - sig)))).astype(bf16)
        du = (grad_h * silu).astype(bf16)
        dg_ref[...] = dg.reshape(dg_ref.shape)
        du_ref[...] = du.reshape(du_ref.shape)
        gx = lax.dot_general(dg, wg_ref[0], nt, preferred_element_type=f32)
        gx = gx + lax.dot_general(du, wu_ref[0], nt, preferred_element_type=f32)
        gx_ref[...] = gx.astype(bf16).reshape(gx_ref.shape)

    wide = pl.BlockSpec((1, chunk, CAP, width), lambda e, c: (e, c, 0, 0))
    narrow = pl.BlockSpec((1, chunk, CAP, hidden), lambda e, c: (e, c, 0, 0))
    level = pl.BlockSpec((1, chunk, CAP, 128), lambda e, c: (e, c, 0, 0))
    column = pl.BlockSpec((1, width, hidden), lambda e, c: (e, 0, 0))
    line = pl.BlockSpec((1, hidden, width), lambda e, c: (e, 0, 0))
    small = jax.ShapeDtypeStruct((experts, groups, CAP, hidden), bf16)
    big = jax.ShapeDtypeStruct(arrived.shape, bf16)
    return pl.pallas_call(
        kernel,
        grid=(experts, groups // chunk),
        in_specs=[wide, wide, level, column, column, line],
        out_specs=[wide, wide, narrow, narrow, narrow],
        out_shape=[big, big, small, small, small],
        name="experts",
    )(arrived, grad_arrived, slot_gate, gate_weight, up_weight, down_weight)


def expert_weight_grads(saved):
    experts, groups, _, width = saved[0][0].shape
    hidden = saved[0][2].shape[-1]
    chunk = math.gcd(groups, 8)
    rows = chunk * CAP
    count = len(saved)

    def kernel(*refs):
        out_refs = refs[5 * count :]
        tn = (((0,), (0,)), ((), ()))

        def total(left, right, left_width, right_width):
            result = None
            for m in range(count):
                a = refs[5 * m + left][...].reshape(rows, left_width)
                b = refs[5 * m + right][...].reshape(rows, right_width)
                part = lax.dot_general(a, b, tn, preferred_element_type=f32)
                result = part if result is None else result + part
            return result

        values = (
            total(0, 3, width, hidden),
            total(0, 4, width, hidden),
            total(2, 1, hidden, width),
        )
        if groups == chunk:
            for ref, value in zip(out_refs, values):
                ref[0] = value
        else:
            first = pl.program_id(1) == 0

            @pl.when(first)
            def _():
                for ref, value in zip(out_refs, values):
                    ref[0] = value

            @pl.when(jnp.logical_not(first))
            def _():
                for ref, value in zip(out_refs, values):
                    ref[0] = ref[0] + value

    wide = pl.BlockSpec((1, chunk, CAP, width), lambda e, c: (e, c, 0, 0))
    narrow = pl.BlockSpec((1, chunk, CAP, hidden), lambda e, c: (e, c, 0, 0))
    column = pl.BlockSpec((1, width, hidden), lambda e, c: (e, 0, 0))
    line = pl.BlockSpec((1, hidden, width), lambda e, c: (e, 0, 0))
    return pl.pallas_call(
        kernel,
        grid=(experts, groups // chunk),
        in_specs=[wide, wide, narrow, narrow, narrow] * count,
        out_specs=[column, column, line],
        out_shape=[
            jax.ShapeDtypeStruct((experts, width, hidden), f32),
            jax.ShapeDtypeStruct((experts, width, hidden), f32),
            jax.ShapeDtypeStruct((experts, hidden, width), f32),
        ],
        name="expert_weight_grads",
    )(*[item for entry in saved for item in entry])


NT = (((1,), (1,)), ((), ()))
TN = (((0,), (0,)), ((), ()))


def masked_scores(query, keys, query_segment, key_segment):
    raw = lax.dot_general(query, keys, NT, preferred_element_type=f32)
    return jnp.where(query_segment == key_segment, raw * scale, mask_value)


def attend_forward(own, other, query_segment, key_segment):
    queries = own.shape[0]
    others = other.shape[0]
    block = math.gcd(queries, 256)

    def kernel(query_ref, own_ref, other_ref, qs_ref, ks_ref, out_ref, log_ref):
        query = query_ref[...]
        segment = qs_ref[...]
        first = masked_scores(query, own_ref[:, HEAD : 2 * HEAD], segment, ks_ref[:, :queries])
        second = masked_scores(query, other_ref[:, :HEAD], segment, ks_ref[:, queries:])
        top = jnp.maximum(
            jnp.max(first, axis=1, keepdims=True), jnp.max(second, axis=1, keepdims=True)
        )
        first = jnp.exp(first - top)
        second = jnp.exp(second - top)
        total = jnp.sum(first, axis=1, keepdims=True) + jnp.sum(second, axis=1, keepdims=True)
        inverse = 1.0 / total
        mixed = jnp.dot(
            (first * inverse).astype(bf16), own_ref[:, 2 * HEAD :], preferred_element_type=f32
        )
        mixed = mixed + jnp.dot(
            (second * inverse).astype(bf16), other_ref[:, HEAD:], preferred_element_type=f32
        )
        out_ref[...] = mixed.astype(bf16)
        log_ref[...] = jnp.broadcast_to(top + jnp.log(total), log_ref.shape)

    return pl.pallas_call(
        kernel,
        grid=(queries // block,),
        in_specs=[
            pl.BlockSpec((block, HEAD), lambda i: (i, 0)),
            pl.BlockSpec(own.shape, lambda i: (0, 0)),
            pl.BlockSpec(other.shape, lambda i: (0, 0)),
            pl.BlockSpec((block, 1), lambda i: (i, 0)),
            pl.BlockSpec((1, queries + others), lambda i: (0, 0)),
        ],
        out_specs=[
            pl.BlockSpec((block, HEAD), lambda i: (i, 0)),
            pl.BlockSpec((block, 128), lambda i: (i, 0)),
        ],
        out_shape=[
            jax.ShapeDtypeStruct((queries, HEAD), bf16),
            jax.ShapeDtypeStruct((queries, 128), f32),
        ],
        name="attend_forward",
    )(own, own, other, query_segment, key_segment)


def attend_backward(own, other, grad_out, log_total, query_segment, key_segment):
    queries = own.shape[0]
    others = other.shape[0]
    block = math.gcd(queries, 256)

    def kernel(
        query_ref, own_ref, other_ref, grad_ref, log_ref, qs_ref, ks_ref, dq_ref, own_out, other_out
    ):
        query = query_ref[...]
        grad = grad_ref[...]
        segment = qs_ref[...]
        log_value = log_ref[:, :1]
        k1 = own_ref[:, HEAD : 2 * HEAD]
        v1 = own_ref[:, 2 * HEAD :]
        k2 = other_ref[:, :HEAD]
        v2 = other_ref[:, HEAD:]
        p1 = jnp.exp(masked_scores(query, k1, segment, ks_ref[:, :queries]) - log_value)
        p2 = jnp.exp(masked_scores(query, k2, segment, ks_ref[:, queries:]) - log_value)
        g1 = lax.dot_general(grad, v1, NT, preferred_element_type=f32)
        g2 = lax.dot_general(grad, v2, NT, preferred_element_type=f32)
        delta = jnp.sum(p1 * g1, axis=1, keepdims=True) + jnp.sum(p2 * g2, axis=1, keepdims=True)
        s1 = (p1 * (g1 - delta) * scale).astype(bf16)
        s2 = (p2 * (g2 - delta) * scale).astype(bf16)
        dq = jnp.dot(s1, k1, preferred_element_type=f32)
        dq = dq + jnp.dot(s2, k2, preferred_element_type=f32)
        dq_ref[...] = dq.astype(bf16)

        @pl.when(pl.program_id(0) == 0)
        def _():
            own_out[...] = jnp.zeros_like(own_out)
            other_out[...] = jnp.zeros_like(other_out)

        own_out[:, :HEAD] += lax.dot_general(s1, query, TN, preferred_element_type=f32)
        own_out[:, HEAD:] += lax.dot_general(p1.astype(bf16), grad, TN, preferred_element_type=f32)
        other_out[:, :HEAD] += lax.dot_general(s2, query, TN, preferred_element_type=f32)
        other_out[:, HEAD:] += lax.dot_general(p2.astype(bf16), grad, TN, preferred_element_type=f32)

    rows = pl.BlockSpec((block, HEAD), lambda i: (i, 0))
    return pl.pallas_call(
        kernel,
        grid=(queries // block,),
        in_specs=[
            rows,
            pl.BlockSpec(own.shape, lambda i: (0, 0)),
            pl.BlockSpec(other.shape, lambda i: (0, 0)),
            rows,
            pl.BlockSpec((block, 128), lambda i: (i, 0)),
            pl.BlockSpec((block, 1), lambda i: (i, 0)),
            pl.BlockSpec((1, queries + others), lambda i: (0, 0)),
        ],
        out_specs=[
            rows,
            pl.BlockSpec((queries, 2 * HEAD), lambda i: (0, 0)),
            pl.BlockSpec((others, 2 * HEAD), lambda i: (0, 0)),
        ],
        out_shape=[
            jax.ShapeDtypeStruct((queries, HEAD), bf16),
            jax.ShapeDtypeStruct((queries, 2 * HEAD), f32),
            jax.ShapeDtypeStruct((others, 2 * HEAD), f32),
        ],
        name="attend_backward",
    )(own, own, other, grad_out, log_total, query_segment, key_segment)


def make_body(n_fsdp, n_tp):
    move = Exchange(n_fsdp, n_tp)

    def body(
        tokens,
        cotangent,
        lengths,
        dealing,
        routes,
        gate_weights,
        attention_gain,
        mixture_gain,
        query_gain,
        key_gain,
        query_weight,
        key_weight,
        value_weight,
        out_weight,
        gate_weight,
        up_weight,
        down_weight,
    ):
        micro, rows, width = tokens.shape
        group = routes.shape[1]
        experts = gate_weight.shape[0]
        f_own = lax.axis_index("fsdp")
        t_own = lax.axis_index("tp")
        inner = query_weight.shape[1]
        heads = inner // HEAD
        sharers = n_fsdp // heads
        head_own = f_own // sharers

        packed = jnp.concatenate([query_weight, key_weight, value_weight], axis=1)
        packed_full = lax.all_gather(packed, "fsdp", axis=0, tiled=True)
        out_full = lax.all_gather(out_weight, "fsdp", axis=0, tiled=True)

        gathered = move.gather_tp(tokens, 1)

        ids = jnp.arange(EXPERTS, dtype=jnp.int32)[None, :, None]
        dense = jnp.zeros((micro, EXPERTS, group), f32)
        for choose in range(TOPK):
            hit = routes[:, None, :, choose] == ids
            dense = dense + jnp.where(hit, gate_weights[:, None, :, choose], 0.0)
        every = lax.all_gather(dense, "fsdp", axis=0, tiled=False)
        mine = lax.dynamic_slice_in_dim(every, f_own * experts, experts, 2)
        mine = relative(mine, 0, f_own)
        mine = relative(
            mine.reshape(n_fsdp, micro, experts, n_tp, rows), 3, t_own
        ).reshape(n_fsdp, micro, experts, group)
        mine = jnp.transpose(mine, (1, 0, 2, 3))
        named = mine > 0.0
        earlier = jnp.triu(jnp.ones((group, group), bf16), 1)
        before = jnp.einsum(
            "mgei,ij->mgej", named.astype(bf16), earlier, preferred_element_type=f32
        )
        slots = jnp.where(named, before.astype(jnp.int32), -1)

        grad_rows = cotangent
        grad_parts = move.gather_fsdp(move.gather_tp(grad_rows, 1), 1)

        dealt = relative(dealing.reshape(micro, n_fsdp, n_tp, rows), 1, f_own)
        dealt = relative(dealt, 2, t_own).reshape(micro, n_fsdp, group)
        order = []
        for lead in range(sharers):
            order += [lead + sharers * p for p in range(heads)]

        def exchange_heads(blocks):
            parts = [blocks[0]] + [
                move.f(blocks[d], d * sharers) for d in range(1, heads)
            ]
            return jnp.stack(parts)

        saved = []

        def forward(m, earlier):
            ordered = jnp.stack([dealt[m, d] for d in order])
            segment, _ = layout(lengths[m], ordered.reshape(-1))
            query_segment = segment[: heads * group].reshape(-1, 1)
            key_segment = segment.reshape(1, -1)
            _, position = layout(lengths[m], dealt[m, 0])
            cosine, sine = angles(position)

            def shape_heads(projected, gain):
                return rotate(head_norm(projected, gain), cosine, sine)

            group_rows = gathered[m]
            if earlier is not None:
                group_rows = after(group_rows, earlier)
            group_rows = group_rows.astype(f32)
            level = lax.rsqrt(
                jnp.mean(group_rows * group_rows, axis=-1, keepdims=True) + norm_epsilon
            )
            plain = group_rows * level
            attn_input = (plain * attention_gain).astype(bf16)
            projected = jnp.dot(attn_input, packed_full, preferred_element_type=f32)
            query_proj = projected[:, :inner].reshape(group, heads, HEAD)
            key_proj = projected[:, inner : 2 * inner].reshape(group, heads, HEAD)
            value_low = projected[:, 2 * inner :].astype(bf16).reshape(group, heads, HEAD)
            query_rot = shape_heads(query_proj, query_gain).astype(bf16)
            key_rot = shape_heads(key_proj, key_gain).astype(bf16)
            bundle = jnp.concatenate([query_rot, key_rot, value_low], axis=2)
            bundle = relative(jnp.transpose(bundle, (1, 0, 2)), 0, head_own)
            own = exchange_heads(bundle).reshape(heads * group, 3 * HEAD)
            own_pair = own[:, HEAD:]
            other = jnp.concatenate([move.f(own_pair, d) for d in range(1, sharers)], axis=0)
            mixed, log_total = attend_forward(own, other, query_segment, key_segment)
            back = relative(exchange_heads(mixed.reshape(heads, group, HEAD)), 0, head_own)
            mixed_low = jnp.transpose(back, (1, 0, 2)).reshape(group, inner)
            attn_part = lax.dot_general(mixed_low, out_full, NT, preferred_element_type=f32)
            state = tokens[m].astype(f32) + move.scatter_tp(attn_part.reshape(n_tp, rows, width))
            normed_two = rms_norm(state, mixture_gain).astype(bf16)
            row_parts = move.gather_fsdp(move.gather_tp(normed_two, 0), 0)
            return dict(
                shape_heads=shape_heads,
                plain=plain,
                attn_input=attn_input,
                query_proj=query_proj,
                key_proj=key_proj,
                own=own,
                other=other,
                log_total=log_total,
                segments=(query_segment, key_segment),
                mixed_low=mixed_low,
                state=state,
                row_parts=row_parts,
            )

        def mixture(m, row_parts, earlier):
            slot = slots[m] if earlier is None else after(slots[m], earlier)
            grad_arrived, slot_gate = dispatch(grad_parts, m, slot, mine[m])
            arrived = dispatch(row_parts, 0, slot, None)
            expert_out, grad_out, hidden, grad_gate, grad_up = experts_step(
                arrived, grad_arrived, slot_gate, gate_weight, up_weight, down_weight
            )
            saved.append((arrived, grad_arrived, hidden, grad_gate, grad_up))
            return expert_out, grad_out

        def to_rows(even, odd):
            parts = move.scatter_fsdp(even, odd)
            return move.scatter_tp(rounded_sum(*parts).reshape(n_tp, rows, width))

        def backward(m, fwd, grad_normed_two):
            state = fwd["state"]
            mixed_low = fwd["mixed_low"]
            shape_heads = fwd["shape_heads"]
            _, pull_two = jax.vjp(rms_norm, state, mixture_gain)
            grad_from_norm, grad_mixture = pull_two(grad_normed_two)
            grad_state = grad_rows[m].astype(f32) + grad_from_norm
            grad_state_group = move.gather_tp(grad_state.astype(bf16), 0)
            out_part = lax.dot_general(grad_state_group, mixed_low, TN, preferred_element_type=f32)
            grad_mixed = jnp.dot(grad_state_group, out_full, preferred_element_type=f32)
            grad_mixed = jnp.transpose(
                grad_mixed.astype(bf16).reshape(group, heads, HEAD), (1, 0, 2)
            )
            grad_heads = exchange_heads(relative(grad_mixed, 0, head_own))
            grad_query, sums_own, sums_other = attend_backward(
                fwd["own"],
                fwd["other"],
                grad_heads.reshape(heads * group, HEAD),
                fwd["log_total"],
                *fwd["segments"],
            )
            sums_other = sums_other.reshape(sharers - 1, heads * group, 2 * HEAD)
            sums = rounded_sum(
                sums_own, *[move.f(sums_other[d - 1], d) for d in range(1, sharers)]
            ).astype(bf16)
            back = jnp.concatenate([grad_query, sums], axis=1).reshape(heads, group, 3 * HEAD)
            back = relative(exchange_heads(back), 0, head_own)
            back = jnp.transpose(back, (1, 0, 2)).astype(f32)
            _, pull_query = jax.vjp(shape_heads, fwd["query_proj"], query_gain)
            grad_query_proj, grad_qgain = pull_query(back[:, :, :HEAD])
            _, pull_key = jax.vjp(shape_heads, fwd["key_proj"], key_gain)
            grad_key_proj, grad_kgain = pull_key(back[:, :, HEAD : 2 * HEAD])
            grad_low = jnp.concatenate(
                [
                    grad_query_proj.reshape(group, inner).astype(bf16),
                    grad_key_proj.reshape(group, inner).astype(bf16),
                    back[:, :, 2 * HEAD :].reshape(group, inner).astype(bf16),
                ],
                axis=1,
            )
            qkv_part = lax.dot_general(
                fwd["attn_input"], grad_low, TN, preferred_element_type=f32
            )
            grad_input_attn = lax.dot_general(
                grad_low, packed_full, NT, preferred_element_type=f32
            )
            grad_attention = jnp.sum(grad_input_attn * fwd["plain"], axis=0)
            grad_normed_one = move.scatter_tp(grad_input_attn.reshape(n_tp, rows, width))
            _, pull_one = jax.vjp(
                lambda value: rms_norm(value, attention_gain), tokens[m].astype(f32)
            )
            (grad_source,) = pull_one(grad_normed_one)
            gains = (grad_attention, grad_mixture, grad_qgain, grad_kgain)
            return grad_state + grad_source, out_part, qkv_part, jnp.concatenate(gains)

        fwds = []
        for m in range(micro):
            fwds.append(forward(m, None))
        expert_outs = []
        row_grads = []
        for m in range(micro):
            later = None
            expert_out, grad_out = mixture(m, fwds[m]["row_parts"], later)
            expert_outs.append(expert_out)
            row_grads.append(combine(grad_out, slots[m]))
        grads_two = [to_rows(*pair) for pair in row_grads]
        outputs = []
        for m in range(micro):
            held = expert_outs[m]
            outputs.append((fwds[m]["state"] + to_rows(*combine(held, slots[m]))).astype(bf16))
        results = [backward(m, fwds[m], grads_two[m]) for m in range(micro)]
        gate_grad, up_grad, down_grad = expert_weight_grads(saved)

        def spread_rows(parts):
            total = parts[0]
            for part in parts[1:]:
                total = total + part
            return lax.psum_scatter(
                total.astype(bf16), "fsdp", scatter_dimension=0, tiled=True
            ).astype(f32)

        out_grad = spread_rows([r[1] for r in results])
        gains = results[0][3]
        for r in results[1:]:
            gains = gains + r[3]
        gains = move.total(gains)
        qkv_grad = spread_rows([r[2] for r in results])
        head = query_gain.shape[0]
        return (
            jnp.stack(outputs),
            jnp.stack([r[0] for r in results]),
            gains[:width],
            gains[width : 2 * width],
            gains[2 * width : 2 * width + head],
            gains[2 * width + head :],
            qkv_grad[:, :inner],
            qkv_grad[:, inner : 2 * inner],
            qkv_grad[:, 2 * inner :],
            out_grad,
            gate_grad,
            up_grad,
            down_grad,
        )

    return body


def solution(mesh):
    weight = P("fsdp", "tp")
    column = P("fsdp", None, "tp")
    line = P("fsdp", "tp", None)
    spread = P(None, ("fsdp", "tp"), None)
    routed = P(None, "fsdp", None)
    in_specs = (
        (spread, spread, P(), P(), routed, routed)
        + (P(),) * 4
        + (weight,) * 4
        + (column, column, line)
    )
    out_specs = (spread, spread) + (P(),) * 4 + (weight,) * 4 + (column, column, line)
    body = make_body(mesh.shape["fsdp"], mesh.shape["tp"])
    return jax.shard_map(body, mesh=mesh, in_specs=in_specs, out_specs=out_specs, check_vma=False)
```

```python
import math

import jax
import jax.numpy as jnp
from jax import lax
from jax.experimental import pallas as pl
from jax.experimental.pallas import tpu as pltpu
from jax.sharding import PartitionSpec as P

HEAD = 128
EXPERTS = 64
TOPK = 8
CAP = 48

norm_epsilon = 1e-05
head_epsilon = 1e-06
rope_base = 50000.0
mask_value = -1e30
scale = HEAD ** (-0.5)
bf16 = jnp.bfloat16
f32 = jnp.float32


def rms_norm(value, gain):
    return value * lax.rsqrt(jnp.mean(value * value, axis=-1, keepdims=True) + norm_epsilon) * gain


def head_norm(value, gain):
    return value * lax.rsqrt(jnp.mean(value * value, axis=-1, keepdims=True) + head_epsilon) * gain


def rotate(value, cosine, sine):
    half = value.shape[-1] // 2
    first = value[..., :half]
    second = value[..., half:]
    return jnp.concatenate(
        [first * cosine - second * sine, second * cosine + first * sine], axis=-1
    )


def angles(position):
    half = HEAD // 2
    rates = rope_base ** (-2.0 * jnp.arange(half, dtype=f32) / HEAD)
    theta = position.astype(f32)[:, None] * rates[None, :]
    return (jnp.cos(theta)[:, None, :], jnp.sin(theta)[:, None, :])


def layout(lengths_row, dealt):
    ends = jnp.cumsum(lengths_row)
    starts = ends - lengths_row
    segment = jnp.sum((dealt[:, None] >= ends[None, :]).astype(jnp.int32), axis=1)
    chosen = segment[:, None] == jnp.arange(lengths_row.shape[0], dtype=jnp.int32)[None, :]
    position = dealt - jnp.sum(jnp.where(chosen, starts[None, :], 0), axis=1)
    return (segment, position)


def relative(value, axis, own):
    size = value.shape[axis]
    bit = 1
    while bit < size:
        shape = value.shape[:axis] + (size // (2 * bit), 2, bit) + value.shape[axis + 1 :]
        split = value.reshape(shape)
        flipped = jnp.flip(split, axis + 1)
        value = jnp.where((own & bit) != 0, flipped, split).reshape(value.shape)
        bit *= 2
    return value


def swap(value, axis_name, size, distance):
    return lax.ppermute(value, axis_name, [(i, i ^ distance) for i in range(size)])


def rounded_sum(*parts):
    total = parts[0].astype(f32)
    for part in parts[1:]:
        total = total + part.astype(f32)
    return total


def after(value, earlier):
    return lax.optimization_barrier((value, earlier))[0]


class Exchange:
    def __init__(self, n_fsdp, n_tp):
        self.n_fsdp = n_fsdp
        self.n_tp = n_tp

    def f(self, value, distance):
        return swap(value, "fsdp", self.n_fsdp, distance)

    def t(self, value, distance):
        return swap(value, "tp", self.n_tp, distance)

    def total(self, value):
        for size, step in ((self.n_tp, self.t), (self.n_fsdp, self.f)):
            distance = 1
            while distance < size:
                value = value + step(value, distance)
                distance *= 2
        return value

    def gather_tp(self, rows, axis):
        parts = [rows] + [self.t(rows, d) for d in range(1, self.n_tp)]
        return jnp.concatenate(parts, axis=axis)

    def scatter_tp(self, blocks):
        low = blocks.astype(bf16)
        return rounded_sum(blocks[0], *[self.t(low[d], d) for d in range(1, self.n_tp)])

    def gather_fsdp(self, rows, axis):
        if self.n_fsdp != 8:
            return [rows] + [self.f(rows, d) for d in range(1, self.n_fsdp)]
        half = rows.shape[axis] // 2
        from_x = self.f(rows, 2)
        from_y = self.f(rows, 4)
        from_core = self.f(rows, 1)
        low = self.f(lax.slice_in_dim(from_y, 0, half, axis=axis), 2)
        high = self.f(lax.slice_in_dim(from_x, half, 2 * half, axis=axis), 4)
        far = jnp.concatenate([low, high], axis=axis)
        return [
            rows,
            from_core,
            from_x,
            self.f(from_x, 1),
            from_y,
            self.f(from_y, 1),
            far,
            self.f(far, 1),
        ]

    def scatter_fsdp(self, even, odd):
        if self.n_fsdp != 8:
            parts = [even[0]]
            for d in range(1, self.n_fsdp):
                source = odd if d % 2 else even
                parts.append(self.f(source[d // 2], d))
            return parts
        both = rounded_sum(even, self.f(odd, 1)).astype(bf16)
        half = both.shape[1] // 2
        low = self.f(both[3, :half], 2)
        high = self.f(both[3, half:], 4)
        to_y = jnp.concatenate(
            [rounded_sum(both[2, :half], low).astype(bf16), both[2, half:]], axis=0
        )
        to_x = jnp.concatenate(
            [both[1, :half], rounded_sum(both[1, half:], high).astype(bf16)], axis=0
        )
        return [both[0], self.f(to_x, 2), self.f(to_y, 4)]


def one_hot(slot):
    experts, rows = slot.shape
    places = lax.broadcasted_iota(jnp.int32, (CAP, rows), 0)
    return jnp.concatenate(
        [
            jnp.where(slot[e : e + 1, :] == places, 1.0, 0.0).astype(bf16)
            for e in range(experts)
        ],
        axis=0,
    )


def dispatch(parts, micro_step, slot, gates):
    groups, experts, rows = slot.shape
    width = parts[0].shape[-1]
    stacked = parts[0].ndim == 3
    scaled = gates is not None

    def kernel(*refs):
        slot_ref = refs[0]
        refs = refs[1:]
        if scaled:
            gate_ref = refs[0]
            refs = refs[1:]
        sources = refs[:groups]
        refs = refs[groups:]
        out_ref = refs[0]
        refs = refs[1:]
        if scaled:
            slot_gate_ref = refs[0]
            refs = refs[1:]
        buffer, semaphore = refs
        step = pl.program_id(0)

        def copy(j, place):
            source = sources[j].at[micro_step] if stacked else sources[j]
            return pltpu.make_async_copy(source, buffer.at[place], semaphore.at[place])

        @pl.when(step == 0)
        def _():
            copy(0, 0).start()

        for j in range(groups):
            @pl.when(step == j)
            def _():
                if j + 1 < groups:
                    copy(j + 1, (j + 1) % 2).start()
                copy(j, j % 2).wait()

        chosen = one_hot(slot_ref[0])
        taken = jnp.dot(chosen, buffer[step % 2], preferred_element_type=f32)
        if scaled:
            wide = jnp.concatenate(
                [jnp.broadcast_to(gate_ref[0, e : e + 1, :], (CAP, rows)) for e in range(experts)],
                axis=0,
            )
            level = jnp.sum(jnp.where(chosen > 0, wide, 0.0), axis=1, keepdims=True)
            taken = taken * level
            slot_gate_ref[...] = jnp.broadcast_to(level, (experts * CAP, 128)).reshape(
                experts, 1, CAP, 128
            )
        out_ref[...] = taken.astype(bf16).reshape(experts, 1, CAP, width)

    small = pl.BlockSpec((1, experts, rows), lambda g: (g, 0, 0))
    out_shape = [jax.ShapeDtypeStruct((experts, groups, CAP, width), bf16)]
    out_specs = [pl.BlockSpec((experts, 1, CAP, width), lambda g: (0, g, 0, 0))]
    if scaled:
        out_shape.append(jax.ShapeDtypeStruct((experts, groups, CAP, 128), f32))
        out_specs.append(pl.BlockSpec((experts, 1, CAP, 128), lambda g: (0, g, 0, 0)))
    operands = [slot] + ([gates] if scaled else []) + list(parts)
    result = pl.pallas_call(
        kernel,
        grid=(groups,),
        in_specs=[small] * (2 if scaled else 1) + [pl.BlockSpec(memory_space=pl.ANY)] * groups,
        out_specs=out_specs,
        out_shape=out_shape,
        scratch_shapes=[pltpu.VMEM((2, rows, width), bf16), pltpu.SemaphoreType.DMA((2,))],
        name="dispatch_grad" if scaled else "dispatch",
    )(*operands)
    return result if scaled else result[0]


def combine(values, slot):
    experts, groups, _, width = values.shape
    rows = slot.shape[-1]

    def kernel(slot_ref, value_ref, even_ref, odd_ref):
        chosen = one_hot(slot_ref[0])
        summed = lax.dot_general(
            chosen,
            value_ref[...].reshape(experts * CAP, width),
            (((0,), (0,)), ((), ())),
            preferred_element_type=f32,
        ).astype(bf16)
        step = pl.program_id(0)

        @pl.when(step % 2 == 0)
        def _():
            even_ref[0] = summed

        @pl.when(step % 2 == 1)
        def _():
            odd_ref[0] = summed

    return pl.pallas_call(
        kernel,
        grid=(groups,),
        in_specs=[
            pl.BlockSpec((1, experts, rows), lambda g: (g, 0, 0)),
            pl.BlockSpec((experts, 1, CAP, width), lambda g: (0, g, 0, 0)),
        ],
        out_specs=[pl.BlockSpec((1, rows, width), lambda g: (g // 2, 0, 0))] * 2,
        out_shape=[jax.ShapeDtypeStruct((groups // 2, rows, width), bf16)] * 2,
        name="combine",
    )(slot, values)


def experts_step(arrived, grad_arrived, slot_gate, gate_weight, up_weight, down_weight):
    experts, groups, _, width = arrived.shape
    hidden = gate_weight.shape[2]
    chunk = math.gcd(groups, 8)
    rows = chunk * CAP

    def kernel(x_ref, g_ref, level_ref, wg_ref, wu_ref, wd_ref, y_ref, gx_ref, h_ref, dg_ref, du_ref):
        x = x_ref[...].reshape(rows, width)
        gate_act = jnp.dot(x, wg_ref[0], preferred_element_type=f32)
        up_act = jnp.dot(x, wu_ref[0], preferred_element_type=f32)
        sig = 1.0 / (1.0 + jnp.exp(-gate_act))
        silu = gate_act * sig
        h = (silu * up_act).astype(bf16)
        h_ref[...] = h.reshape(h_ref.shape)
        y = jnp.dot(h, wd_ref[0], preferred_element_type=f32)
        level = level_ref[...].reshape(rows, 128)[:, :1]
        y_ref[...] = (y * level).astype(bf16).reshape(y_ref.shape)
        g = g_ref[...].reshape(rows, width)
        nt = (((1,), (1,)), ((), ()))
        grad_h = lax.dot_general(g, wd_ref[0], nt, preferred_element_type=f32)
        dg = (grad_h * up_act * (sig * (1.0 + gate_act * (1.0 - sig)))).astype(bf16)
        du = (grad_h * silu).astype(bf16)
        dg_ref[...] = dg.reshape(dg_ref.shape)
        du_ref[...] = du.reshape(du_ref.shape)
        gx = lax.dot_general(dg, wg_ref[0], nt, preferred_element_type=f32)
        gx = gx + lax.dot_general(du, wu_ref[0], nt, preferred_element_type=f32)
        gx_ref[...] = gx.astype(bf16).reshape(gx_ref.shape)

    wide = pl.BlockSpec((1, chunk, CAP, width), lambda e, c: (e, c, 0, 0))
    narrow = pl.BlockSpec((1, chunk, CAP, hidden), lambda e, c: (e, c, 0, 0))
    level = pl.BlockSpec((1, chunk, CAP, 128), lambda e, c: (e, c, 0, 0))
    column = pl.BlockSpec((1, width, hidden), lambda e, c: (e, 0, 0))
    line = pl.BlockSpec((1, hidden, width), lambda e, c: (e, 0, 0))
    small = jax.ShapeDtypeStruct((experts, groups, CAP, hidden), bf16)
    big = jax.ShapeDtypeStruct(arrived.shape, bf16)
    return pl.pallas_call(
        kernel,
        grid=(experts, groups // chunk),
        in_specs=[wide, wide, level, column, column, line],
        out_specs=[wide, wide, narrow, narrow, narrow],
        out_shape=[big, big, small, small, small],
        name="experts",
    )(arrived, grad_arrived, slot_gate, gate_weight, up_weight, down_weight)


def expert_weight_grads(saved):
    experts, groups, _, width = saved[0][0].shape
    hidden = saved[0][2].shape[-1]
    chunk = math.gcd(groups, 8)
    rows = chunk * CAP
    count = len(saved)

    def kernel(*refs):
        out_refs = refs[5 * count :]
        tn = (((0,), (0,)), ((), ()))

        def total(left, right, left_width, right_width):
            result = None
            for m in range(count):
                a = refs[5 * m + left][...].reshape(rows, left_width)
                b = refs[5 * m + right][...].reshape(rows, right_width)
                part = lax.dot_general(a, b, tn, preferred_element_type=f32)
                result = part if result is None else result + part
            return result

        values = (
            total(0, 3, width, hidden),
            total(0, 4, width, hidden),
            total(2, 1, hidden, width),
        )
        if groups == chunk:
            for ref, value in zip(out_refs, values):
                ref[0] = value
        else:
            first = pl.program_id(1) == 0

            @pl.when(first)
            def _():
                for ref, value in zip(out_refs, values):
                    ref[0] = value

            @pl.when(jnp.logical_not(first))
            def _():
                for ref, value in zip(out_refs, values):
                    ref[0] = ref[0] + value

    wide = pl.BlockSpec((1, chunk, CAP, width), lambda e, c: (e, c, 0, 0))
    narrow = pl.BlockSpec((1, chunk, CAP, hidden), lambda e, c: (e, c, 0, 0))
    column = pl.BlockSpec((1, width, hidden), lambda e, c: (e, 0, 0))
    line = pl.BlockSpec((1, hidden, width), lambda e, c: (e, 0, 0))
    return pl.pallas_call(
        kernel,
        grid=(experts, groups // chunk),
        in_specs=[wide, wide, narrow, narrow, narrow] * count,
        out_specs=[column, column, line],
        out_shape=[
            jax.ShapeDtypeStruct((experts, width, hidden), f32),
            jax.ShapeDtypeStruct((experts, width, hidden), f32),
            jax.ShapeDtypeStruct((experts, hidden, width), f32),
        ],
        name="expert_weight_grads",
        cost_estimate=pl.CostEstimate(
            flops=6 * count * experts * groups * CAP * width * hidden,
            transcendentals=0,
            bytes_accessed=experts * width * (4 * count * groups * CAP + 12 * hidden),
        ),
    )(*[item for entry in saved for item in entry])


NT = (((1,), (1,)), ((), ()))
TN = (((0,), (0,)), ((), ()))


def masked_scores(query, keys, query_segment, key_segment):
    raw = lax.dot_general(query, keys, NT, preferred_element_type=f32)
    return jnp.where(query_segment == key_segment, raw * scale, mask_value)


def attend_forward(own, other, query_segment, key_segment):
    queries = own.shape[0]
    others = other.shape[0]
    block = math.gcd(queries, 256)

    def kernel(query_ref, own_ref, other_ref, qs_ref, ks_ref, out_ref, log_ref):
        query = query_ref[...]
        segment = qs_ref[...]
        first = masked_scores(query, own_ref[:, HEAD : 2 * HEAD], segment, ks_ref[:, :queries])
        second = masked_scores(query, other_ref[:, :HEAD], segment, ks_ref[:, queries:])
        top = jnp.maximum(
            jnp.max(first, axis=1, keepdims=True), jnp.max(second, axis=1, keepdims=True)
        )
        first = jnp.exp(first - top)
        second = jnp.exp(second - top)
        total = jnp.sum(first, axis=1, keepdims=True) + jnp.sum(second, axis=1, keepdims=True)
        inverse = 1.0 / total
        mixed = jnp.dot(
            (first * inverse).astype(bf16), own_ref[:, 2 * HEAD :], preferred_element_type=f32
        )
        mixed = mixed + jnp.dot(
            (second * inverse).astype(bf16), other_ref[:, HEAD:], preferred_element_type=f32
        )
        out_ref[...] = mixed.astype(bf16)
        log_ref[...] = jnp.broadcast_to(top + jnp.log(total), log_ref.shape)

    return pl.pallas_call(
        kernel,
        grid=(queries // block,),
        in_specs=[
            pl.BlockSpec((block, HEAD), lambda i: (i, 0)),
            pl.BlockSpec(own.shape, lambda i: (0, 0)),
            pl.BlockSpec(other.shape, lambda i: (0, 0)),
            pl.BlockSpec((block, 1), lambda i: (i, 0)),
            pl.BlockSpec((1, queries + others), lambda i: (0, 0)),
        ],
        out_specs=[
            pl.BlockSpec((block, HEAD), lambda i: (i, 0)),
            pl.BlockSpec((block, 128), lambda i: (i, 0)),
        ],
        out_shape=[
            jax.ShapeDtypeStruct((queries, HEAD), bf16),
            jax.ShapeDtypeStruct((queries, 128), f32),
        ],
        name="attend_forward",
    )(own, own, other, query_segment, key_segment)


def attend_backward(own, other, grad_out, log_total, query_segment, key_segment):
    queries = own.shape[0]
    others = other.shape[0]
    block = math.gcd(queries, 256)

    def kernel(
        query_ref, own_ref, other_ref, grad_ref, log_ref, qs_ref, ks_ref, dq_ref, own_out, other_out
    ):
        query = query_ref[...]
        grad = grad_ref[...]
        segment = qs_ref[...]
        log_value = log_ref[:, :1]
        k1 = own_ref[:, HEAD : 2 * HEAD]
        v1 = own_ref[:, 2 * HEAD :]
        k2 = other_ref[:, :HEAD]
        v2 = other_ref[:, HEAD:]
        p1 = jnp.exp(masked_scores(query, k1, segment, ks_ref[:, :queries]) - log_value)
        p2 = jnp.exp(masked_scores(query, k2, segment, ks_ref[:, queries:]) - log_value)
        g1 = lax.dot_general(grad, v1, NT, preferred_element_type=f32)
        g2 = lax.dot_general(grad, v2, NT, preferred_element_type=f32)
        delta = jnp.sum(p1 * g1, axis=1, keepdims=True) + jnp.sum(p2 * g2, axis=1, keepdims=True)
        s1 = (p1 * (g1 - delta) * scale).astype(bf16)
        s2 = (p2 * (g2 - delta) * scale).astype(bf16)
        dq = jnp.dot(s1, k1, preferred_element_type=f32)
        dq = dq + jnp.dot(s2, k2, preferred_element_type=f32)
        dq_ref[...] = dq.astype(bf16)

        @pl.when(pl.program_id(0) == 0)
        def _():
            own_out[...] = jnp.zeros_like(own_out)
            other_out[...] = jnp.zeros_like(other_out)

        own_out[:, :HEAD] += lax.dot_general(s1, query, TN, preferred_element_type=f32)
        own_out[:, HEAD:] += lax.dot_general(p1.astype(bf16), grad, TN, preferred_element_type=f32)
        other_out[:, :HEAD] += lax.dot_general(s2, query, TN, preferred_element_type=f32)
        other_out[:, HEAD:] += lax.dot_general(p2.astype(bf16), grad, TN, preferred_element_type=f32)

    rows = pl.BlockSpec((block, HEAD), lambda i: (i, 0))
    return pl.pallas_call(
        kernel,
        grid=(queries // block,),
        in_specs=[
            rows,
            pl.BlockSpec(own.shape, lambda i: (0, 0)),
            pl.BlockSpec(other.shape, lambda i: (0, 0)),
            rows,
            pl.BlockSpec((block, 128), lambda i: (i, 0)),
            pl.BlockSpec((block, 1), lambda i: (i, 0)),
            pl.BlockSpec((1, queries + others), lambda i: (0, 0)),
        ],
        out_specs=[
            rows,
            pl.BlockSpec((queries, 2 * HEAD), lambda i: (0, 0)),
            pl.BlockSpec((others, 2 * HEAD), lambda i: (0, 0)),
        ],
        out_shape=[
            jax.ShapeDtypeStruct((queries, HEAD), bf16),
            jax.ShapeDtypeStruct((queries, 2 * HEAD), f32),
            jax.ShapeDtypeStruct((others, 2 * HEAD), f32),
        ],
        name="attend_backward",
    )(own, own, other, grad_out, log_total, query_segment, key_segment)


def make_body(n_fsdp, n_tp):
    move = Exchange(n_fsdp, n_tp)

    def body(
        tokens,
        cotangent,
        lengths,
        dealing,
        routes,
        gate_weights,
        attention_gain,
        mixture_gain,
        query_gain,
        key_gain,
        query_weight,
        key_weight,
        value_weight,
        out_weight,
        gate_weight,
        up_weight,
        down_weight,
    ):
        micro, rows, width = tokens.shape
        group = routes.shape[1]
        experts = gate_weight.shape[0]
        f_own = lax.axis_index("fsdp")
        t_own = lax.axis_index("tp")
        inner = query_weight.shape[1]
        heads = inner // HEAD
        sharers = n_fsdp // heads
        head_own = f_own // sharers

        packed = jnp.concatenate([query_weight, key_weight, value_weight], axis=1)
        packed_full = lax.all_gather(packed, "fsdp", axis=0, tiled=True)
        out_full = lax.all_gather(out_weight, "fsdp", axis=0, tiled=True)

        normed_one = move.gather_tp(rms_norm(tokens.astype(f32), attention_gain).astype(bf16), 1)

        ids = jnp.arange(EXPERTS, dtype=jnp.int32)[None, :, None]
        dense = jnp.zeros((micro, EXPERTS, group), f32)
        for choose in range(TOPK):
            hit = routes[:, None, :, choose] == ids
            dense = dense + jnp.where(hit, gate_weights[:, None, :, choose], 0.0)
        every = lax.all_gather(dense, "fsdp", axis=0, tiled=False)
        mine = lax.dynamic_slice_in_dim(every, f_own * experts, experts, 2)
        mine = relative(mine, 0, f_own)
        mine = relative(
            mine.reshape(n_fsdp, micro, experts, n_tp, rows), 3, t_own
        ).reshape(n_fsdp, micro, experts, group)
        mine = jnp.transpose(mine, (1, 0, 2, 3))
        named = mine > 0.0
        earlier = jnp.triu(jnp.ones((group, group), bf16), 1)
        before = jnp.einsum(
            "mgei,ij->mgej", named.astype(bf16), earlier, preferred_element_type=f32
        )
        slots = jnp.where(named, before.astype(jnp.int32), -1)

        grad_rows = cotangent
        grad_parts = move.gather_fsdp(move.gather_tp(grad_rows, 1), 1)

        dealt = relative(dealing.reshape(micro, n_fsdp, n_tp, rows), 1, f_own)
        dealt = relative(dealt, 2, t_own).reshape(micro, n_fsdp, group)
        order = []
        for lead in range(sharers):
            order += [lead + sharers * p for p in range(heads)]

        def exchange_heads(blocks):
            parts = [blocks[0]] + [
                move.f(blocks[d], d * sharers) for d in range(1, heads)
            ]
            return jnp.stack(parts)

        saved = []

        def forward(m, earlier):
            ordered = jnp.stack([dealt[m, d] for d in order])
            segment, _ = layout(lengths[m], ordered.reshape(-1))
            query_segment = segment[: heads * group].reshape(-1, 1)
            key_segment = segment.reshape(1, -1)
            _, position = layout(lengths[m], dealt[m, 0])
            cosine, sine = angles(position)

            def shape_heads(projected, gain):
                return rotate(head_norm(projected, gain), cosine, sine)

            attn_input = normed_one[m]
            projected = jnp.dot(attn_input, packed_full, preferred_element_type=f32)
            query_proj = projected[:, :inner].reshape(group, heads, HEAD)
            key_proj = projected[:, inner : 2 * inner].reshape(group, heads, HEAD)
            value_low = projected[:, 2 * inner :].astype(bf16).reshape(group, heads, HEAD)
            query_rot = shape_heads(query_proj, query_gain).astype(bf16)
            key_rot = shape_heads(key_proj, key_gain).astype(bf16)
            bundle = jnp.concatenate([query_rot, key_rot, value_low], axis=2)
            bundle = relative(jnp.transpose(bundle, (1, 0, 2)), 0, head_own)
            own = exchange_heads(bundle).reshape(heads * group, 3 * HEAD)
            own_pair = own[:, HEAD:]
            other = jnp.concatenate([move.f(own_pair, d) for d in range(1, sharers)], axis=0)
            mixed, log_total = attend_forward(own, other, query_segment, key_segment)
            back = relative(exchange_heads(mixed.reshape(heads, group, HEAD)), 0, head_own)
            mixed_low = jnp.transpose(back, (1, 0, 2)).reshape(group, inner)
            attn_part = lax.dot_general(mixed_low, out_full, NT, preferred_element_type=f32)
            state = tokens[m].astype(f32) + move.scatter_tp(attn_part.reshape(n_tp, rows, width))
            normed_two = rms_norm(state, mixture_gain).astype(bf16)
            row_parts = move.gather_fsdp(move.gather_tp(normed_two, 0), 0)
            return dict(
                shape_heads=shape_heads,
                attn_input=attn_input,
                query_proj=query_proj,
                key_proj=key_proj,
                own=own,
                other=other,
                log_total=log_total,
                segments=(query_segment, key_segment),
                mixed_low=mixed_low,
                state=state,
                row_parts=row_parts,
            )

        def mixture(m, row_parts, earlier):
            slot = slots[m] if earlier is None else after(slots[m], earlier)
            grad_arrived, slot_gate = dispatch(grad_parts, m, slot, mine[m])
            arrived = dispatch(row_parts, 0, slot, None)
            expert_out, grad_out, hidden, grad_gate, grad_up = experts_step(
                arrived, grad_arrived, slot_gate, gate_weight, up_weight, down_weight
            )
            saved.append((arrived, grad_arrived, hidden, grad_gate, grad_up))
            return expert_out, grad_out

        def to_rows(even, odd):
            parts = move.scatter_fsdp(even, odd)
            return move.scatter_tp(rounded_sum(*parts).reshape(n_tp, rows, width))

        def backward(m, fwd, grad_normed_two):
            state = fwd["state"]
            mixed_low = fwd["mixed_low"]
            shape_heads = fwd["shape_heads"]
            _, pull_two = jax.vjp(rms_norm, state, mixture_gain)
            grad_from_norm, grad_mixture = pull_two(grad_normed_two)
            grad_state = grad_rows[m].astype(f32) + grad_from_norm
            grad_state_group = move.gather_tp(grad_state.astype(bf16), 0)
            out_part = lax.dot_general(grad_state_group, mixed_low, TN, preferred_element_type=f32)
            grad_mixed = jnp.dot(grad_state_group, out_full, preferred_element_type=f32)
            grad_mixed = jnp.transpose(
                grad_mixed.astype(bf16).reshape(group, heads, HEAD), (1, 0, 2)
            )
            grad_heads = exchange_heads(relative(grad_mixed, 0, head_own))
            grad_query, sums_own, sums_other = attend_backward(
                fwd["own"],
                fwd["other"],
                grad_heads.reshape(heads * group, HEAD),
                fwd["log_total"],
                *fwd["segments"],
            )
            sums_other = sums_other.reshape(sharers - 1, heads * group, 2 * HEAD)
            sums = rounded_sum(
                sums_own, *[move.f(sums_other[d - 1], d) for d in range(1, sharers)]
            ).astype(bf16)
            back = jnp.concatenate([grad_query, sums], axis=1).reshape(heads, group, 3 * HEAD)
            back = relative(exchange_heads(back), 0, head_own)
            back = jnp.transpose(back, (1, 0, 2)).astype(f32)
            _, pull_query = jax.vjp(shape_heads, fwd["query_proj"], query_gain)
            grad_query_proj, grad_qgain = pull_query(back[:, :, :HEAD])
            _, pull_key = jax.vjp(shape_heads, fwd["key_proj"], key_gain)
            grad_key_proj, grad_kgain = pull_key(back[:, :, HEAD : 2 * HEAD])
            grad_low = jnp.concatenate(
                [
                    grad_query_proj.reshape(group, inner).astype(bf16),
                    grad_key_proj.reshape(group, inner).astype(bf16),
                    back[:, :, 2 * HEAD :].reshape(group, inner).astype(bf16),
                ],
                axis=1,
            )
            qkv_part = lax.dot_general(
                fwd["attn_input"], grad_low, TN, preferred_element_type=f32
            )
            grad_input_attn = lax.dot_general(
                grad_low, packed_full, NT, preferred_element_type=f32
            )
            grad_attention = (
                jnp.sum(grad_input_attn * fwd["attn_input"].astype(f32), axis=0) / attention_gain
            )
            grad_normed_one = move.scatter_tp(grad_input_attn.reshape(n_tp, rows, width))
            _, pull_one = jax.vjp(
                lambda value: rms_norm(value, attention_gain), tokens[m].astype(f32)
            )
            (grad_source,) = pull_one(grad_normed_one)
            gains = (grad_attention, grad_mixture, grad_qgain, grad_kgain)
            low_input = grad_input_attn
            return grad_state + grad_source, out_part, qkv_part, jnp.concatenate(gains), low_input

        fwds = []
        for m in range(micro):
            fwds.append(forward(m, None))
        expert_outs = []
        row_grads = []
        for m in range(micro):
            later = None
            expert_out, grad_out = mixture(m, fwds[m]["row_parts"], later)
            expert_outs.append(expert_out)
            row_grads.append(combine(grad_out, slots[m]))
        grads_two = [to_rows(*pair) for pair in row_grads]
        outputs = []
        for m in range(micro):
            held = expert_outs[m]
            outputs.append((fwds[m]["state"] + to_rows(*combine(held, slots[m]))).astype(bf16))
        results = [backward(m, fwds[m], grads_two[m]) for m in range(micro)]
        saved[-1] = saved[-1][:-1] + (after(saved[-1][-1], results[-1][4]),)
        gate_grad, up_grad, down_grad = expert_weight_grads(saved)

        def spread_rows(parts):
            total = parts[0]
            for part in parts[1:]:
                total = total + part
            return lax.psum_scatter(
                total.astype(bf16), "fsdp", scatter_dimension=0, tiled=True
            ).astype(f32)

        out_grad = spread_rows([r[1] for r in results])
        gains = results[0][3]
        for r in results[1:]:
            gains = gains + r[3]
        gains = move.total(gains)
        qkv_grad = spread_rows([r[2] for r in results])
        head = query_gain.shape[0]
        return (
            jnp.stack(outputs),
            jnp.stack([r[0] for r in results]),
            gains[:width],
            gains[width : 2 * width],
            gains[2 * width : 2 * width + head],
            gains[2 * width + head :],
            qkv_grad[:, :inner],
            qkv_grad[:, inner : 2 * inner],
            qkv_grad[:, 2 * inner :],
            out_grad,
            gate_grad,
            up_grad,
            down_grad,
        )

    return body


def solution(mesh):
    weight = P("fsdp", "tp")
    column = P("fsdp", None, "tp")
    line = P("fsdp", "tp", None)
    spread = P(None, ("fsdp", "tp"), None)
    routed = P(None, "fsdp", None)
    in_specs = (
        (spread, spread, P(), P(), routed, routed)
        + (P(),) * 4
        + (weight,) * 4
        + (column, column, line)
    )
    out_specs = (spread, spread) + (P(),) * 4 + (weight,) * 4 + (column, column, line)
    body = make_body(mesh.shape["fsdp"], mesh.shape["tp"])
    return jax.shard_map(body, mesh=mesh, in_specs=in_specs, out_specs=out_specs, check_vma=False)
```
